128 devices in a mesh: line: 16 (over y, x), col: 8 (over z, core).
Axes of the slice: x: 4, y: 4, z: 4, core: 2. Of those that a mesh axis runs over, the one named last changes fastest.
Arguments:
- fields: float32 [4, 512, 64, 512], P(None, 'line', 'col'), may hold values from -4 to 4
- viscosity: float32 [512, 64, 512], P('line', 'col'), may hold values from 0.5 to 2
Outputs:
- updated: float32 [4, 512, 64, 512], P(None, 'line', 'col')
The draws below stay inside these ranges and needn't reach their ends.
All inputs are finite; a program needn't handle non-finite values.
Results may differ from the reference program's by a relative error of at most 0.0003.
Values sent between devices are 32-bit elements; how exact they have to be, the bound alone decides.
A program may use at most 64 MiB of HBM per device.

```python
import math
import jax
import jax.numpy as jnp
from jax import lax

NX = 512
NY = 64
NZ = 512
STIFF = 3072


def draw_fields(key, part):
    shape = (4, NX, NY, NZ)
    rough_key, mode_key = jax.random.split(key)
    x_coord = (jnp.arange(NX, dtype=jnp.float32) + 0.5) / NX
    rough = jax.random.truncated_normal(rough_key, -2.5, 2.5, shape, jnp.float32)
    amounts = jax.random.uniform(mode_key, (3, 4, 1, NY, NZ), jnp.float32, -0.5, 0.5)
    first_mode = jnp.sin(math.pi * x_coord)[None, :, None, None]
    second_mode = jnp.sin(2.0 * math.pi * x_coord)[None, :, None, None]
    third_mode = jnp.sin(3.0 * math.pi * x_coord)[None, :, None, None]
    smooth = amounts[0] * first_mode + amounts[1] * second_mode + amounts[2] * third_mode
    return rough + smooth


def block_scale(rng, dims, cuts, smallest, top_value):
    def one(axis_at, shards_of):
        heights = jax.random.uniform(jax.random.fold_in(jax.random.fold_in(rng, 6), axis_at), (shards_of,), jnp.float32, smallest / len(cuts), top_value / len(cuts))
        return jnp.repeat(jnp.exp(heights), dims[axis_at] // shards_of).reshape((-1,) + (1,) * (len(dims) - axis_at - 1))

    level = one(*cuts[0])
    for cut in cuts[1:]:
        level = level * one(*cut)
    return level


def setup_inputs(seed: int = 0) -> dict:
    keys = jax.random.split(jax.random.key(seed), 3)
    return {
        "fields": draw_fields(jax.random.fold_in(keys[2], 71), 0),
        "viscosity": jnp.clip(jnp.exp(math.log(2.0) - 1.3862944 * jax.random.uniform(keys[1], (NX, NY, NZ), jnp.float32) ** block_scale(keys[1], (NX, NY, NZ), ((0, 16), (1, 8)), -0.2, 0.2)), 0.5, 2.0),
    }


THERMAL_RATIO = 0.8
CROSS_RATE = 0.2
ADVECTION = 0.25
BUOYANCY = 2.0


def neighbours(values, along, wrapped):
    length = values.shape[along]
    widths = [(0, 0)] * values.ndim
    widths[along] = (1, 1)
    if wrapped:
        padded = jnp.pad(values, widths, mode="wrap")
    else:
        padded = jnp.pad(values, widths, mode="constant")
    upper = lax.slice_in_dim(padded, 2, length + 2, axis=along)
    lower = lax.slice_in_dim(padded, 0, length, axis=along)
    return upper, lower


def thomas(sub_diag, diagonal, super_diag, source):
    initial = jnp.zeros(source.shape[1:], source.dtype)

    def forward(state, record):
        prev_upper, prev_source = state
        sub_row, diag_row, super_row, source_row = record
        divisor = diag_row - sub_row * prev_upper
        next_upper = super_row / divisor
        next_source = (source_row - sub_row * prev_source) / divisor
        return (next_upper, next_source), (next_upper, next_source)

    _, (uppers, sources) = lax.scan(forward, (initial, initial), (sub_diag, diagonal, super_diag, source))

    def backward(following, record):
        upper_row, source_row = record
        solved = source_row - upper_row * following
        return solved, solved

    _, solved = lax.scan(backward, initial, (uppers, sources), reverse=True)
    return solved


def reference(fields, viscosity):
    directions = ((0, False), (1, True), (2, False))
    face_list = []
    for along, wrapped in directions:
        visc_next, visc_prev = neighbours(viscosity, along, wrapped)
        face_list.append((0.5 * (viscosity + visc_next), 0.5 * (viscosity + visc_prev)))
    results = []
    for member in range(4):
        field = fields[member]
        weight = THERMAL_RATIO if member == 3 else 1.0
        diffusions = []
        centrals = []
        for along, wrapped in directions:
            field_next, field_prev = neighbours(field, along, wrapped)
            face_next, face_prev = face_list[along]
            diffusions.append(face_next * (field_next - field) - face_prev * (field - field_prev))
            centrals.append(0.5 * (field_next - field_prev))
        transport = fields[0] * centrals[0] + fields[1] * centrals[1] + fields[2] * centrals[2]
        source = field + weight * (CROSS_RATE * diffusions[1] + CROSS_RATE * diffusions[2]) - ADVECTION * transport
        if member == 2:
            source = source + BUOYANCY * fields[3]
        rate = STIFF * weight
        low_side = rate * face_list[0][1]
        high_side = rate * face_list[0][0]
        results.append(thomas(-low_side, 1.0 + low_side + high_side, -high_side, source))
    return jnp.stack(results)
```

```python
import functools

import jax
import jax.numpy as jnp
from jax import lax
from jax.experimental import pallas as pl
from jax.experimental.pallas import tpu as pltpu
from jax.sharding import PartitionSpec as P

STIFF = 3072.0
THERMAL_RATIO = 0.8
CROSS_RATE = 0.2
ADVECTION = 0.25
BUOYANCY = 2.0
MESH = pl.DeviceIdType.MESH
LANES = 128
SIDE = 4


def rates(q):
    return 0.5 * STIFF * (1.0 if q == 0 else THERMAL_RATIO)


def main_kernel(
    lines, cols, rows, chunks,
    f_hbm, v_hbm,
    y_out, m_out, w_out, b_out,
    fv, src, rec, mass, halo_out, halo_in,
    mat_out, mat_in, rhs_out, rhs_in, sep, bounds, pivots,
    load_sem, x_send, x_recv, y_send, y_recv,
    mat_send, mat_recv, rhs_send, rhs_recv, sep_send, sep_recv, plane_sem,
):
    me = lax.axis_index("line")
    col = lax.axis_index("col")
    right, left = lax.rem(me + 1, lines), lax.rem(me + lines - 1, lines)
    above, below = lax.rem(col + 1, cols), lax.rem(col + cols - 1, cols)
    row_of, place = me // SIDE, lax.rem(me, SIDE)
    last = rows - 1

    barrier = pltpu.get_barrier_semaphore()
    row_peers = [row_of * SIDE + lax.rem(place + d, SIDE) for d in range(1, SIDE)]
    column_peers = [lax.rem(row_of + d, lines // SIDE) * SIDE + place for d in range(1, lines // SIDE)]
    greeted = [{"line": p} for p in row_peers + column_peers + [right, left]]
    greeted += [{"col": above}, {"col": below}]
    for peer in greeted:
        pl.semaphore_signal(barrier, inc=1, device_id=peer, device_id_type=MESH)

    loads = []
    for c in range(chunks):
        lanes = pl.ds(c * LANES, LANES)
        own = pl.ds(1, rows)
        loads.append((
            pltpu.make_async_copy(v_hbm.at[:, :, lanes], fv.at[4, c, own], load_sem.at[c, 0]),
            pltpu.make_async_copy(f_hbm.at[:, :, :, lanes], fv.at[pl.ds(0, 4), c, own], load_sem.at[c, 1]),
        ))
    for pair in loads:
        pair[0].start()
        pair[1].start()

    for c in range(chunks):
        loads[c][0].wait()
        loads[c][1].wait()
        for a in range(5):
            for side, y in ((0, 7), (1, 0)):
                for g in range(0, rows, 8):
                    halo_out[side, c, a, g : g + 8, :] = fv[a, c, 1 + g : 9 + g, y, :]

    pl.semaphore_wait(barrier, len(greeted))

    to_right = pltpu.make_async_remote_copy(
        fv.at[:, :, rows], fv.at[:, :, 0], x_send.at[0], x_recv.at[0],
        device_id={"line": right}, device_id_type=MESH)
    to_left = pltpu.make_async_remote_copy(
        fv.at[pl.ds(0, 4), :, 1], fv.at[pl.ds(0, 4), :, rows + 1], x_send.at[1], x_recv.at[1],
        device_id={"line": left}, device_id_type=MESH)
    to_right.start()
    to_left.start()
    y_copies = []
    for c in range(chunks):
        pair = []
        for side, peer in ((0, above), (1, below)):
            copy = pltpu.make_async_remote_copy(
                halo_out.at[side, c], halo_in.at[side, c], y_send.at[side, c], y_recv.at[side, c],
                device_id={"col": peer}, device_id_type=MESH)
            copy.start()
            pair.append(copy)
        y_copies.append(pair)
    for peer in column_peers:
        pl.semaphore_signal(plane_sem, inc=1, device_id={"line": peer}, device_id_type=MESH)

    def matrix_step(k, carry):
        new = []
        for c in range(chunks):
            total = fv[4, c, k + 1] + fv[4, c, k]
            for q in range(2):
                h, e, mass_right = carry[2 * c + q]
                a = rates(q) * total
                r = 1.0 / (a + (h + e))
                m = a * r
                w = e * r
                rec[q, c, k] = r
                m_out[q, c, k] = m
                w_out[q, c, k] = w
                new.append((1.0 + m * h, m * e, mass_right + w * h))
        return tuple(new)

    start = []
    for c in range(chunks):
        total = fv[4, c, rows] + fv[4, c, rows - 1]
        for q in range(2):
            a = rates(q) * total
            start.append((jnp.ones_like(a), a, jnp.zeros_like(a)))
    state = lax.fori_loop(0, last - 1, lambda i, s: matrix_step(last - 1 - i, s), tuple(start))
    for c in range(chunks):
        for q in range(2):
            for n in range(3):
                mass[q, c, n] = state[2 * c + q][n]

    shape = (8, LANES)
    lane = lax.broadcasted_iota(jnp.int32, shape, 1)
    level = lax.broadcasted_iota(jnp.int32, shape, 0)
    z_first, z_last = lane == 0, lane == LANES - 1
    y_first, y_last = level == 0, level == 7

    def z_pair(values):
        ahead = [pltpu.roll(x, LANES - 1, 1) for x in values] + [jnp.zeros(shape, jnp.float32)]
        behind = [jnp.zeros(shape, jnp.float32)] + [pltpu.roll(x, 1, 1) for x in values]
        z_next = [jnp.where(z_last, ahead[c + 1], ahead[c]) for c in range(chunks)]
        z_prev = [jnp.where(z_first, behind[c], behind[c + 1]) for c in range(chunks)]
        return z_next, z_prev

    def source_row(p):
        visc = [fv[4, c, p] for c in range(chunks)]
        z_next, z_prev = z_pair(visc)
        half = 0.5 * CROSS_RATE
        az_next = [half * (visc[c] + z_next[c]) for c in range(chunks)]
        az_prev = [half * (visc[c] + z_prev[c]) for c in range(chunks)]
        ay_next = [jnp.where(y_last, 0.0, half * (visc[c] + pltpu.roll(visc[c], 7, 0))) for c in range(chunks)]
        ay_prev = [jnp.where(y_first, 0.0, half * (visc[c] + pltpu.roll(visc[c], 1, 0))) for c in range(chunks)]
        speed = [[(0.5 * ADVECTION) * fv[a, c, p] for c in range(chunks)] for a in range(3)]
        for a in range(4):
            own = [fv[a, c, p] for c in range(chunks)]
            z_next, z_prev = z_pair(own)
            for c in range(chunks):
                f = own[c]
                y_next = jnp.where(y_last, 0.0, pltpu.roll(f, 7, 0))
                y_prev = jnp.where(y_first, 0.0, pltpu.roll(f, 1, 0))
                spread = az_next[c] * (z_next[c] - f) - az_prev[c] * (f - z_prev[c])
                spread += ay_next[c] * (y_next - f) - ay_prev[c] * (f - y_prev)
                carried = speed[0][c] * (fv[a, c, p + 1] - fv[a, c, p - 1])
                carried += speed[1][c] * (y_next - y_prev) + speed[2][c] * (z_next[c] - z_prev[c])
                total = f + (THERMAL_RATIO * spread if a == 3 else spread) - carried
                if a == 2:
                    total += BUOYANCY * fv[3, c, p]
                src[a, c, p - 1] = total

    def source_step(p, nothing):
        source_row(p)
        return nothing

    lax.fori_loop(2, rows, source_step, 0)

    to_right.wait_recv()
    to_left.wait_recv()

    @pl.when(me == 0)
    def _():
        fv[:, :, 0] = jnp.zeros((5, chunks) + shape, jnp.float32)

    @pl.when(me == lines - 1)
    def _():
        fv[0:4, :, rows + 1] = jnp.zeros((4, chunks) + shape, jnp.float32)

    source_row(1)
    source_row(rows)

    at_end = jnp.where(me == lines - 1, 1.0, 0.0)
    for c in range(chunks):
        total = fv[4, c, 1] + fv[4, c, 0]
        wall = at_end * fv[4, c, rows]
        for q in range(2):
            h, e, mass_right = (mass[q, c, n] for n in range(3))
            a = rates(q) * total
            r = 1.0 / (a + (h + e))
            m = a * r
            w = e * r
            rec[q, c, 0] = r
            m_out[q, c, 0] = m
            w_out[q, c, 0] = w
            mat_out[c, q, 0] = m * e
            mat_out[c, q, 1] = m * h
            mat_out[c, q, 2] = 1.0 + mass_right + w * h + rates(q) * wall

    pl.semaphore_wait(plane_sem, len(column_peers))

    def mat_copy(owner):
        c, a = owner // 4, lax.rem(owner, 4)
        return pltpu.make_async_remote_copy(
            mat_out.at[c, a // 3], mat_in.at[me], mat_send.at[owner], mat_recv.at[me],
            device_id={"line": owner}, device_id_type=MESH)

    def mat_start(d, nothing):
        mat_copy(lax.rem(me + d, lines)).start()
        return nothing

    lax.fori_loop(1, lines, mat_start, 0)
    mat_in[me] = mat_out[me // 4, lax.rem(me, 4) // 3]

    edge = jnp.where(y_first | y_last, 0.5 * CROSS_RATE, 0.0)
    sign = jnp.where(y_last, -0.5 * ADVECTION, jnp.where(y_first, 0.5 * ADVECTION, 0.0))

    def rhs_copy(owner):
        return pltpu.make_async_remote_copy(
            rhs_out.at[owner], rhs_in.at[me], rhs_send.at[owner], rhs_recv.at[me],
            device_id={"line": owner}, device_id_type=MESH)

    for c in range(chunks):
        for copy in y_copies[c]:
            copy.wait_recv()

        def finished(k):
            def beyond(a):
                low = jnp.broadcast_to(halo_in[0, c, a, pl.ds(k, 1), :], shape)
                high = jnp.broadcast_to(halo_in[1, c, a, pl.ds(k, 1), :], shape)
                return jnp.where(y_last, high, low)

            face = edge * (fv[4, c, k + 1] + beyond(4))
            speed = sign * fv[1, c, k + 1]
            out = []
            for a in range(4):
                outer = beyond(a)
                spread = face * (outer - fv[a, c, k + 1])
                if a == 3:
                    spread = THERMAL_RATIO * spread
                out.append(src[a, c, k] + (spread + speed * outer))
            return out

        def rhs_step(i, carry):
            k = last - 1 - i
            given = finished(k)
            new = []
            for a in range(4):
                q = a // 3
                passed, gathered = carry[a]
                d = given[a] + passed
                y_out[a, c, k] = rec[q, c, k] * d
                new.append((m_out[q, c, k] * d, gathered + w_out[q, c, k] * d))
            return tuple(new)

        at_last = finished(last)
        zero = jnp.zeros(shape, jnp.float32)
        ends = lax.fori_loop(0, last, rhs_step, tuple((zero, at_last[a]) for a in range(4)))
        for a in range(4):
            rhs_out[4 * c + a, 0] = ends[a][0]
            rhs_out[4 * c + a, 1] = ends[a][1]

        for a in range(4):
            owner = 4 * c + a

            @pl.when(me != owner)
            def _(owner=owner):
                rhs_copy(owner).start()

    rhs_in[me] = rhs_out[me]

    def mat_wait(d, nothing):
        j = lax.rem(me + d, lines)
        pltpu.make_async_remote_copy(
            mat_out.at[0, 0], mat_in.at[j], mat_send.at[j], mat_recv.at[j],
            device_id={"line": j}, device_id_type=MESH).wait_recv()
        return nothing

    lax.fori_loop(1, lines, mat_wait, 0)

    def pivot_step(j, before):
        e = mat_in[j, 0]
        r = 1.0 / (e + before)
        m = e * r
        pivots[j, 0] = r
        pivots[j, 1] = m
        ahead = jnp.minimum(j + 1, lines - 1)
        own_mass = mat_in[j, 2] + jnp.where(j + 1 < lines, 1.0, 0.0) * mat_in[ahead, 1]
        return own_mass + m * before

    first = mat_in[0, 0] + (mat_in[0, 2] + mat_in[1, 1])
    final = lax.fori_loop(1, lines, pivot_step, first)
    final = 1.0 / final

    def rhs_wait(d, nothing):
        j = lax.rem(me + d, lines)
        pltpu.make_async_remote_copy(
            rhs_out.at[j], rhs_in.at[j], rhs_send.at[j], rhs_recv.at[j],
            device_id={"line": j}, device_id_type=MESH).wait_recv()
        return nothing

    lax.fori_loop(1, lines, rhs_wait, 0)
    given = [rhs_in[j, 1] + rhs_in[j + 1, 0] if j + 1 < lines else rhs_in[j, 1] for j in range(lines)]
    for j in range(1, lines):
        given[j] = given[j] + pivots[j, 1] * given[j - 1]
    value = final * given[lines - 1]
    sep[0] = jnp.zeros(shape, jnp.float32)
    sep[lines] = value
    for j in range(lines - 1, 0, -1):
        value = pivots[j, 0] * given[j - 1] + pivots[j, 1] * value
        sep[j] = value

    def sep_copy(j):
        return pltpu.make_async_remote_copy(
            sep.at[pl.ds(j, 2)], bounds.at[me], sep_send.at[j], sep_recv.at[me],
            device_id={"line": j}, device_id_type=MESH)

    def sep_start(d, nothing):
        sep_copy(lax.rem(me + d, lines)).start()
        return nothing

    lax.fori_loop(1, lines, sep_start, 0)
    bounds[me] = sep[pl.ds(me, 2)]

    to_right.wait_send()
    to_left.wait_send()
    for pair in y_copies:
        for copy in pair:
            copy.wait_send()
    for owner in range(lines):

        @pl.when(me != owner)
        def _(owner=owner):
            rhs_copy(owner).wait_send()

    def sent(d, nothing):
        j = lax.rem(me + d, lines)
        mat_copy(j).wait_send()
        sep_copy(j).wait_send()
        return nothing

    lax.fori_loop(1, lines, sent, 0)

    def sep_wait(d, nothing):
        j = lax.rem(me + d, lines)
        pltpu.make_async_remote_copy(
            sep.at[pl.ds(0, 2)], bounds.at[j], sep_send.at[j], sep_recv.at[j],
            device_id={"line": j}, device_id_type=MESH).wait_recv()
        return nothing

    lax.fori_loop(1, lines, sep_wait, 0)
    b_out[...] = bounds[...]


def back_kernel(rows, chunks, y, m, w, b, out, buf, sem):
    last = rows - 1
    copies = []
    for c in range(chunks):
        ends = [b[4 * c + a, 1] for a in range(4)]

        def step(k, before):
            new = []
            for a in range(4):
                q = a // 3
                u = y[a, c, k] + m[q, c, k] * before[a] + w[q, c, k] * ends[a]
                buf[a, c, k] = u
                new.append(u)
            return tuple(new)

        lax.fori_loop(0, last, step, tuple(b[4 * c + a, 0] for a in range(4)))
        for a in range(4):
            buf[a, c, last] = ends[a]
        copy = pltpu.make_async_copy(buf.at[:, c], out.at[:, :, :, pl.ds(c * LANES, LANES)], sem.at[c])
        copy.start()
        copies.append(copy)
    for copy in copies:
        copy.wait()


def in_place(array):
    return pltpu.with_memory_space_constraint(array, pltpu.HBM)


def solution(mesh):
    lines, cols = mesh.shape["line"], mesh.shape["col"]

    def local(fields, viscosity):
        _, rows, deep, wide = fields.shape
        chunks = wide // LANES
        assert deep == 8 and 4 * chunks == lines
        f32 = jnp.float32
        tile = (8, LANES)
        vmem = pl.BlockSpec(memory_space=pltpu.VMEM)
        anywhere = pl.BlockSpec(memory_space=pl.ANY)
        dma = pltpu.SemaphoreType.DMA
        y, m, w, b = pl.pallas_call(
            functools.partial(main_kernel, lines, cols, rows, chunks),
            out_shape=(
                jax.ShapeDtypeStruct((4, chunks, rows) + tile, f32),
                jax.ShapeDtypeStruct((2, chunks, rows) + tile, f32),
                jax.ShapeDtypeStruct((2, chunks, rows) + tile, f32),
                jax.ShapeDtypeStruct((lines, 2) + tile, f32),
            ),
            in_specs=[anywhere, anywhere],
            out_specs=(vmem, vmem, vmem, vmem),
            scratch_shapes=[
                pltpu.VMEM((5, chunks, rows + 2) + tile, f32),
                pltpu.VMEM((4, chunks, rows) + tile, f32),
                pltpu.VMEM((2, chunks, rows) + tile, f32),
                pltpu.VMEM((2, chunks, 3) + tile, f32),
                pltpu.VMEM((2, chunks, 5, rows, LANES), f32),
                pltpu.VMEM((2, chunks, 5, rows, LANES), f32),
                pltpu.VMEM((chunks, 2, 3) + tile, f32),
                pltpu.VMEM((lines, 3) + tile, f32),
                pltpu.VMEM((lines, 2) + tile, f32),
                pltpu.VMEM((lines, 2) + tile, f32),
                pltpu.VMEM((lines + 1,) + tile, f32),
                pltpu.VMEM((lines, 2) + tile, f32),
                pltpu.VMEM((lines, 2) + tile, f32),
                dma((chunks, 2)),
                dma((2,)), dma((2,)), dma((2, chunks)), dma((2, chunks)),
                dma((lines,)), dma((lines,)), dma((lines,)), dma((lines,)), dma((lines,)), dma((lines,)),
                pltpu.SemaphoreType.REGULAR,
            ],
            compiler_params=pltpu.CompilerParams(
                collective_id=0, has_side_effects=True, vmem_limit_bytes=40 << 20
            ),
            name="eliminate",
        )(in_place(fields), in_place(viscosity))
        return pl.pallas_call(
            functools.partial(back_kernel, rows, chunks),
            out_shape=jax.ShapeDtypeStruct((4, rows, 8, wide), f32),
            in_specs=[vmem, vmem, vmem, vmem],
            out_specs=anywhere,
            scratch_shapes=[pltpu.VMEM((4, chunks, rows) + tile, f32), dma((chunks,))],
            compiler_params=pltpu.CompilerParams(vmem_limit_bytes=24 << 20),
            name="substitute",
        )(y, m, w, b)

    return jax.shard_map(
        local,
        mesh=mesh,
        in_specs=(P(None, "line", "col", None), P("line", "col", None)),
        out_specs=P(None, "line", "col", None),
        check_vma=False,
    )
```

```python
import functools

import jax
import jax.numpy as jnp
from jax import lax
from jax.experimental import pallas as pl
from jax.experimental.pallas import tpu as pltpu
from jax.sharding import PartitionSpec as P

STIFF = 3072.0
THERMAL_RATIO = 0.8
CROSS_RATE = 0.2
ADVECTION = 0.25
BUOYANCY = 2.0
MESH = pl.DeviceIdType.MESH
LANES = 128
STEP = 6
SIDE = 4


def rates(q):
    return 0.5 * STIFF * (1.0 if q == 0 else THERMAL_RATIO)


def owner_of(c, a):
    near_x, near_y, high_x, high_y = c % 2, c // 2, a % 2, a // 2
    x = (2 + near_x) if high_x else (1 - near_x)
    y = (2 + near_y) if high_y else (1 - near_y)
    return y * SIDE + x


def slot_of(me):
    x, y = lax.rem(me, SIDE), me // SIDE
    high_x, high_y = x // 2, y // 2
    near_x = jnp.where(high_x == 1, x - 2, 1 - x)
    near_y = jnp.where(high_y == 1, y - 2, 1 - y)
    return near_x + 2 * near_y, high_x + 2 * high_y


def main_kernel(
    lines, cols, rows, chunks,
    f_hbm, v_hbm,
    u_out, y_end, m_end, w_end, b_out,
    fv, src, y_all, m_all, w_all, rec, mass, x_left, x_right, halo_in,
    mat_out, mat_in, rhs_out, rhs_in, sep, bounds, pivots,
    load_sem, x_send, x_recv, y_send, y_recv,
    mat_send, mat_recv, rhs_send, rhs_recv, sep_send, sep_recv, plane_sem,
):
    me = lax.axis_index("line")
    col = lax.axis_index("col")
    right, left = lax.rem(me + 1, lines), lax.rem(me + lines - 1, lines)
    above, below = lax.rem(col + 1, cols), lax.rem(col + cols - 1, cols)
    row_of, place = me // SIDE, lax.rem(me, SIDE)
    my_chunk, my_field = slot_of(me)
    my_slot = 4 * my_chunk + my_field
    last = rows - 1
    shape = (8, LANES)
    y_ref = [y_all.at[c] for c in range(chunks - 1)] + [y_end]
    m_ref = [m_all.at[c] for c in range(chunks - 1)] + [m_end]
    w_ref = [w_all.at[c] for c in range(chunks - 1)] + [w_end]

    barrier = pltpu.get_barrier_semaphore()
    row_peers = [row_of * SIDE + lax.rem(place + d, SIDE) for d in range(1, SIDE)]
    column_peers = [lax.rem(row_of + d, lines // SIDE) * SIDE + place for d in range(1, lines // SIDE)]
    greeted = [{"col": above}, {"col": below}]
    greeted += [{"line": p} for p in [right, left] + row_peers + column_peers]
    for peer in greeted:
        pl.semaphore_signal(barrier, inc=1, device_id=peer, device_id_type=MESH)

    loads = []
    own = pl.ds(1, rows)
    for c in range(chunks):
        lanes = pl.ds(c * LANES, LANES)
        loads.append(pltpu.make_async_copy(v_hbm.at[:, :, lanes], fv.at[4, c, own], load_sem.at[c, 0]))
    for c in range(chunks):
        lanes = pl.ds(c * LANES, LANES)
        loads.append(pltpu.make_async_copy(f_hbm.at[:, :, :, lanes], fv.at[pl.ds(0, 4), c, own], load_sem.at[c, 1]))
    for copy in loads:
        copy.start()

    pl.semaphore_wait(barrier, len(greeted))

    def x_copy(n, source, target, peer):
        return pltpu.make_async_remote_copy(
            source, target, x_send.at[n], x_recv.at[n], device_id={"line": peer}, device_id_type=MESH)

    x_copies = [
        x_copy(0, v_hbm.at[last], x_left.at[4], right),
        x_copy(1, f_hbm.at[:, last], x_left.at[pl.ds(0, 4)], right),
        x_copy(2, f_hbm.at[:, 0], x_right, left),
    ]
    for copy in x_copies:
        copy.start()
    y_copies = []
    for c in range(chunks):
        lanes = pl.ds(c * LANES, LANES)
        group = []
        for side, y, peer in ((0, 7, above), (1, 0, below)):
            for n, source, target in (
                (0, f_hbm.at[:, :, y, lanes], halo_in.at[side, c, pl.ds(0, 4)]),
                (1, v_hbm.at[:, y, lanes], halo_in.at[side, c, 4]),
            ):
                copy = pltpu.make_async_remote_copy(
                    source, target, y_send.at[side, c, n], y_recv.at[side, c, n],
                    device_id={"col": peer}, device_id_type=MESH)
                copy.start()
                group.append(copy)
        y_copies.append(group)
    for peer in column_peers:
        pl.semaphore_signal(plane_sem, inc=1, device_id={"line": peer}, device_id_type=MESH)

    for c in range(chunks):
        loads[c].wait()

    def matrix_row(c, q, k, a, h, e):
        r = 1.0 / (a + (h + e))
        m = a * r
        w = e * r
        rec[q, c, k] = r
        m_ref[c][q, k] = m
        w_ref[c][q, k] = w
        return m, w

    def matrix_step(i, carry):
        k = last - 1 - i
        new = []
        for c in range(chunks):
            total = fv[4, c, k + 1] + fv[4, c, k]
            for q in range(2):
                h, e, mass_right = carry[2 * c + q]
                m, w = matrix_row(c, q, k, rates(q) * total, h, e)
                new.append((1.0 + m * h, m * e, mass_right + w * h))
        return tuple(new)

    start = []
    for c in range(chunks):
        total = fv[4, c, rows] + fv[4, c, rows - 1]
        for q in range(2):
            a = rates(q) * total
            start.append((jnp.ones_like(a), a, jnp.zeros_like(a)))
    state = lax.fori_loop(0, last - 1, matrix_step, tuple(start))
    for c in range(chunks):
        for q in range(2):
            for n in range(3):
                mass[q, c, n] = state[2 * c + q][n]

    for c in range(chunks):
        loads[chunks + c].wait()
    lane = lax.broadcasted_iota(jnp.int32, shape, 1)
    level = lax.broadcasted_iota(jnp.int32, shape, 0)
    z_first, z_last = lane == 0, lane == LANES - 1
    y_first, y_last = level == 0, level == 7
    drift = 0.5 * ADVECTION
    inner_next = jnp.where(y_last, 0.0, drift)
    inner_prev = jnp.where(y_first, 0.0, drift)

    def source_row(p):
        half = 0.5 * CROSS_RATE
        zero = jnp.zeros(shape, jnp.float32)
        value = [[fv[a, c, p] if a < 4 else half * fv[4, c, p] for c in range(chunks)] for a in range(5)]
        ahead = [[pltpu.roll(x, LANES - 1, 1) for x in value[a]] + [zero] for a in range(5)]
        behind = [[zero] + [pltpu.roll(x, 1, 1) for x in value[a]] for a in range(5)]
        for c in range(chunks):

            def around(a):
                x = value[a][c]
                z_next = jnp.where(z_last, ahead[a][c + 1], ahead[a][c])
                z_prev = jnp.where(z_first, behind[a][c], behind[a][c + 1])
                return z_next, z_prev, pltpu.roll(x, 7, 0), pltpu.roll(x, 1, 0)

            v = value[4][c]
            z_next, z_prev, y_next, y_prev = around(4)
            face = [v + z_next, v + z_prev, jnp.where(y_last, 0.0, v + y_next), jnp.where(y_first, 0.0, v + y_prev)]
            around_all = (face[0] + face[1]) + (face[2] + face[3])
            speed_x = drift * value[0][c]
            speed_z = drift * value[2][c]
            speed = [-speed_z, speed_z, -(inner_next * value[1][c]), inner_prev * value[1][c]]
            weights = [[face[n] + speed[n] for n in range(4)], [THERMAL_RATIO * face[n] + speed[n] for n in range(4)]]
            centre = [1.0 - around_all, 1.0 - THERMAL_RATIO * around_all]
            for a in range(4):
                q = a // 3
                near = around(a)
                total = centre[q] * value[a][c] - speed_x * (fv[a, c, p + 1] - fv[a, c, p - 1])
                total += (weights[q][0] * near[0] + weights[q][1] * near[1]) + (
                    weights[q][2] * near[2] + weights[q][3] * near[3]
                )
                if a == 2:
                    total += BUOYANCY * value[3][c]
                src[a, c, p - 1] = total

    def source_step(p, nothing):
        source_row(p)
        return nothing

    lax.fori_loop(2, 2 + rows // 2, source_step, 0)

    x_copies[0].wait_recv()
    inside_left = jnp.where(me == 0, 0.0, 1.0)
    inside_right = jnp.where(me == lines - 1, 0.0, 1.0)
    for c in range(chunks):
        total = fv[4, c, 1] + inside_left * x_left[4, :, pl.ds(c * LANES, LANES)]
        wall = (1.0 - inside_right) * fv[4, c, rows]
        for q in range(2):
            h, e, mass_right = (mass[q, c, n] for n in range(3))
            m, w = matrix_row(c, q, 0, rates(q) * total, h, e)
            mat_out[c, q, 0] = m * e
            mat_out[c, q, 1] = m * h
            mat_out[c, q, 2] = 1.0 + mass_right + w * h + rates(q) * wall

    pl.semaphore_wait(plane_sem, len(column_peers))

    def mat_copy(c, a):
        return pltpu.make_async_remote_copy(
            mat_out.at[c, a // 3], mat_in.at[me], mat_send.at[4 * c + a], mat_recv.at[me],
            device_id={"line": owner_of(c, a)}, device_id_type=MESH)

    slots = [(c, a) for c in range(chunks) for a in range(4)]
    for c, a in slots:

        @pl.when(me != owner_of(c, a))
        def _(c=c, a=a):
            mat_copy(c, a).start()

    mat_in[me] = mat_out[my_chunk, my_field // 3]

    lax.fori_loop(2 + rows // 2, rows, source_step, 0)

    x_copies[1].wait_recv()
    x_copies[2].wait_recv()
    for c in range(chunks):
        lanes = pl.ds(c * LANES, LANES)
        for a in range(4):
            fv[a, c, 0] = inside_left * x_left[a, :, lanes]
            fv[a, c, rows + 1] = inside_right * x_right[a, :, lanes]
    source_row(1)
    source_row(rows)

    edge = jnp.where(y_first | y_last, 0.5 * CROSS_RATE, 0.0)
    sign = jnp.where(y_last, -drift, jnp.where(y_first, drift, 0.0))

    def rhs_copy(c, a):
        return pltpu.make_async_remote_copy(
            rhs_out.at[4 * c + a], rhs_in.at[me], rhs_send.at[4 * c + a], rhs_recv.at[me],
            device_id={"line": owner_of(c, a)}, device_id_type=MESH)

    for c in range(chunks):
        for copy in y_copies[c]:
            copy.wait_recv()

        def finished(k):
            def beyond(a):
                low = jnp.broadcast_to(halo_in[0, c, a, pl.ds(k, 1), :], shape)
                high = jnp.broadcast_to(halo_in[1, c, a, pl.ds(k, 1), :], shape)
                return jnp.where(y_last, high, low)

            face = edge * (fv[4, c, k + 1] + beyond(4))
            speed = sign * fv[1, c, k + 1]
            faces = (face, THERMAL_RATIO * face)
            weights = (faces[0] + speed, faces[1] + speed)
            out = []
            for a in range(4):
                q = a // 3
                out.append(src[a, c, k] + (weights[q] * beyond(a) - faces[q] * fv[a, c, k + 1]))
            return out

        def rhs_row(k, carry):
            given = finished(k)
            new = []
            for a in range(4):
                q = a // 3
                passed, gathered = carry[a]
                d = given[a] + passed
                y_ref[c][a, k] = rec[q, c, k] * d
                new.append((m_ref[c][q, k] * d, gathered + w_ref[c][q, k] * d))
            return tuple(new)

        def rhs_step(i, carry):
            for n in range(STEP):
                carry = rhs_row(last - 2 - STEP * i - n, carry)
            return carry

        at_last = finished(last)
        zero = jnp.zeros(shape, jnp.float32)
        ends = rhs_row(last - 1, tuple((zero, at_last[a]) for a in range(4)))
        assert (last - 1) % STEP == 0
        ends = lax.fori_loop(0, (last - 1) // STEP, rhs_step, ends)
        for a in range(4):
            rhs_out[4 * c + a, 0] = ends[a][0]
            rhs_out[4 * c + a, 1] = ends[a][1]

        for a in range(4):

            @pl.when(me != owner_of(c, a))
            def _(c=c, a=a):
                rhs_copy(c, a).start()

    rhs_in[me] = rhs_out[my_slot]

    def arrival(source, target, recv, j):
        return pltpu.make_async_remote_copy(
            source, target.at[j], rhs_send.at[0], recv.at[j], device_id={"line": left}, device_id_type=MESH)

    def mat_wait(d, nothing):
        arrival(mat_out.at[0, 0], mat_in, mat_recv, lax.rem(me + d, lines)).wait_recv()
        return nothing

    lax.fori_loop(1, lines, mat_wait, 0)

    def pivot_step(j, before):
        e = mat_in[j, 0]
        r = 1.0 / (e + before)
        m = e * r
        pivots[j, 0] = r
        pivots[j, 1] = m
        ahead = jnp.minimum(j + 1, lines - 1)
        own_mass = mat_in[j, 2] + jnp.where(j + 1 < lines, 1.0, 0.0) * mat_in[ahead, 1]
        return own_mass + m * before

    first = mat_in[0, 0] + (mat_in[0, 2] + mat_in[1, 1])
    final = lax.fori_loop(1, lines, pivot_step, first)
    final = 1.0 / final

    def rhs_wait(d, nothing):
        arrival(rhs_out.at[0], rhs_in, rhs_recv, lax.rem(me + d, lines)).wait_recv()
        return nothing

    lax.fori_loop(1, lines, rhs_wait, 0)
    given = [rhs_in[j, 1] + rhs_in[j + 1, 0] if j + 1 < lines else rhs_in[j, 1] for j in range(lines)]
    for j in range(1, lines):
        given[j] = given[j] + pivots[j, 1] * given[j - 1]
    value = final * given[lines - 1]
    sep[0] = jnp.zeros(shape, jnp.float32)
    sep[lines] = value
    for j in range(lines - 1, 0, -1):
        value = pivots[j, 0] * given[j - 1] + pivots[j, 1] * value
        sep[j] = value

    def sep_copy(j):
        return pltpu.make_async_remote_copy(
            sep.at[pl.ds(j, 2)], bounds.at[my_slot], sep_send.at[j], sep_recv.at[my_slot],
            device_id={"line": j}, device_id_type=MESH)

    for j in range(lines):

        @pl.when(me != j)
        def _(j=j):
            sep_copy(j).start()

    bounds[my_slot] = sep[pl.ds(me, 2)]

    for copy in x_copies + [copy for group in y_copies for copy in group]:
        copy.wait_send()
    for c, a in slots:

        @pl.when(me != owner_of(c, a))
        def _(c=c, a=a):
            mat_copy(c, a).wait_send()
            rhs_copy(c, a).wait_send()

    for c in range(chunks):
        for a in range(4):

            @pl.when(me != owner_of(c, a))
            def _(c=c, a=a):
                arrival(sep.at[pl.ds(0, 2)], bounds, sep_recv, 4 * c + a).wait_recv()

        if c < chunks - 1:
            substitute(
                last, y_ref[c], m_ref[c], w_ref[c],
                [(bounds[4 * c + a, 0], bounds[4 * c + a, 1]) for a in range(4)], u_out.at[c])
        else:
            for a in range(4):
                b_out[a] = bounds[4 * c + a]

    for j in range(lines):

        @pl.when(me != j)
        def _(j=j):
            sep_copy(j).wait_send()


def substitute(last, y, m, w, ends, out):
    def row(k, before):
        new = []
        for a in range(4):
            q = a // 3
            u = (y[a, k] + w[q, k] * ends[a][1]) + m[q, k] * before[a]
            out[a, k] = u
            new.append(u)
        return tuple(new)

    def step(i, before):
        for n in range(STEP):
            before = row(1 + STEP * i + n, before)
        return before

    assert (last - 1) % STEP == 0
    first = row(0, tuple(end[0] for end in ends))
    lax.fori_loop(0, (last - 1) // STEP, step, first)
    for a in range(4):
        out[a, last] = ends[a][1]


def back_kernel(rows, chunks, u, y, m, w, b, out, buf, sem):
    copies = []

    def write(c, source):
        copy = pltpu.make_async_copy(source, out.at[:, :, :, pl.ds(c * LANES, LANES)], sem.at[c])
        copy.start()
        copies.append(copy)

    for c in range(chunks - 1):
        write(c, u.at[c])
    substitute(rows - 1, y, m, w, [(b[a, 0], b[a, 1]) for a in range(4)], buf)
    write(chunks - 1, buf)
    for copy in copies:
        copy.wait()


def in_place(array):
    return pltpu.with_memory_space_constraint(array, pltpu.HBM)


def solution(mesh):
    lines, cols = mesh.shape["line"], mesh.shape["col"]

    def local(fields, viscosity):
        _, rows, deep, wide = fields.shape
        chunks = wide // LANES
        assert deep == 8 and 4 * chunks == lines
        f32 = jnp.float32
        tile = (8, LANES)
        vmem = pl.BlockSpec(memory_space=pltpu.VMEM)
        anywhere = pl.BlockSpec(memory_space=pl.ANY)
        dma = pltpu.SemaphoreType.DMA
        parts = pl.pallas_call(
            functools.partial(main_kernel, lines, cols, rows, chunks),
            out_shape=(
                jax.ShapeDtypeStruct((chunks - 1, 4, rows) + tile, f32),
                jax.ShapeDtypeStruct((4, rows) + tile, f32),
                jax.ShapeDtypeStruct((2, rows) + tile, f32),
                jax.ShapeDtypeStruct((2, rows) + tile, f32),
                jax.ShapeDtypeStruct((4, 2) + tile, f32),
            ),
            in_specs=[anywhere, anywhere],
            out_specs=(vmem,) * 5,
            scratch_shapes=[
                pltpu.VMEM((5, chunks, rows + 2) + tile, f32),
                pltpu.VMEM((4, chunks, rows) + tile, f32),
                pltpu.VMEM((chunks - 1, 4, rows) + tile, f32),
                pltpu.VMEM((chunks - 1, 2, rows) + tile, f32),
                pltpu.VMEM((chunks - 1, 2, rows) + tile, f32),
                pltpu.VMEM((2, chunks, rows) + tile, f32),
                pltpu.VMEM((2, chunks, 3) + tile, f32),
                pltpu.VMEM((5, deep, wide), f32),
                pltpu.VMEM((4, deep, wide), f32),
                pltpu.VMEM((2, chunks, 5, rows, LANES), f32),
                pltpu.VMEM((chunks, 2, 3) + tile, f32),
                pltpu.VMEM((lines, 3) + tile, f32),
                pltpu.VMEM((lines, 2) + tile, f32),
                pltpu.VMEM((lines, 2) + tile, f32),
                pltpu.VMEM((lines + 1,) + tile, f32),
                pltpu.VMEM((lines, 2) + tile, f32),
                pltpu.VMEM((lines, 2) + tile, f32),
                dma((chunks, 2)),
                dma((3,)), dma((3,)), dma((2, chunks, 2)), dma((2, chunks, 2)),
                dma((lines,)), dma((lines,)), dma((lines,)), dma((lines,)), dma((lines,)), dma((lines,)),
                pltpu.SemaphoreType.REGULAR,
            ],
            compiler_params=pltpu.CompilerParams(
                collective_id=0, has_side_effects=True, vmem_limit_bytes=40 << 20
            ),
            name="eliminate",
        )(in_place(fields), in_place(viscosity))
        return pl.pallas_call(
            functools.partial(back_kernel, rows, chunks),
            out_shape=jax.ShapeDtypeStruct((4, rows, 8, wide), f32),
            in_specs=[vmem] * 5,
            out_specs=anywhere,
            scratch_shapes=[pltpu.VMEM((4, rows) + tile, f32), dma((chunks,))],
            compiler_params=pltpu.CompilerParams(vmem_limit_bytes=24 << 20),
            name="substitute",
        )(*parts)

    return jax.shard_map(
        local,
        mesh=mesh,
        in_specs=(P(None, "line", "col", None), P("line", "col", None)),
        out_specs=P(None, "line", "col", None),
        check_vma=False,
    )
```

```python
import functools

import jax
import jax.numpy as jnp
from jax import lax
from jax.experimental import pallas as pl
from jax.experimental.pallas import tpu as pltpu
from jax.sharding import PartitionSpec as P

STIFF = 3072.0
THERMAL_RATIO = 0.8
CROSS_RATE = 0.2
ADVECTION = 0.25
BUOYANCY = 2.0
MESH = pl.DeviceIdType.MESH
LANES = 128
STEP = 15
TRIP = 5
EARLY = 2
SIDE = 4


def rates(q):
    return 0.5 * STIFF * (1.0 if q == 0 else THERMAL_RATIO)


def owner_of(c, a):
    near_x, near_y, high_x, high_y = c % 2, c // 2, a % 2, a // 2
    x = (2 + near_x) if high_x else (1 - near_x)
    y = (2 + near_y) if high_y else (1 - near_y)
    return y * SIDE + x


def slot_of(me):
    x, y = lax.rem(me, SIDE), me // SIDE
    high_x, high_y = x // 2, y // 2
    near_x = jnp.where(high_x == 1, x - 2, 1 - x)
    near_y = jnp.where(high_y == 1, y - 2, 1 - y)
    return near_x + 2 * near_y, high_x + 2 * high_y


def main_kernel(
    lines, cols, rows, chunks,
    f_hbm, v_hbm,
    u_out, y_end, m_end, w_end, b_out,
    fv, src, y_all, m_all, w_all, rec, mass, x_left, x_right, halo_in,
    mat_out, mat_in, rhs_out, rhs_in, sep, bounds, pivots,
    load_sem, x_send, x_recv, y_send, y_recv,
    mat_send, mat_recv, rhs_send, rhs_recv, sep_send, sep_recv, plane_sem, ready_sem,
):
    me = lax.axis_index("line")
    col = lax.axis_index("col")
    right, left = lax.rem(me + 1, lines), lax.rem(me + lines - 1, lines)
    above, below = lax.rem(col + 1, cols), lax.rem(col + cols - 1, cols)
    row_of, place = me // SIDE, lax.rem(me, SIDE)
    my_chunk, my_field = slot_of(me)
    my_slot = 4 * my_chunk + my_field
    last = rows - 1
    shape = (8, LANES)
    y_ref = [y_all.at[c] for c in range(chunks - 1)] + [y_end]
    m_ref = [m_all.at[c] for c in range(chunks - 1)] + [m_end]
    w_ref = [w_all.at[c] for c in range(chunks - 1)] + [w_end]

    barrier = pltpu.get_barrier_semaphore()
    row_peers = [row_of * SIDE + lax.rem(place + d, SIDE) for d in range(1, SIDE)]
    column_peers = [lax.rem(row_of + d, lines // SIDE) * SIDE + place for d in range(1, lines // SIDE)]
    greeted = [{"line": p} for p in [right, left] + row_peers + column_peers]
    for peer in greeted:
        pl.semaphore_signal(barrier, inc=1, device_id=peer, device_id_type=MESH)
    odd = lax.rem(col, 2) == 1

    @pl.when(jnp.logical_not(odd))
    def _():
        for peer in (above, below):
            pl.semaphore_signal(barrier, inc=1, device_id={"col": peer}, device_id_type=MESH)

    loads = []
    own = pl.ds(1, rows)
    for c in range(chunks):
        lanes = pl.ds(c * LANES, LANES)
        loads.append(pltpu.make_async_copy(v_hbm.at[:, :, lanes], fv.at[4, c, own], load_sem.at[c, 0]))
    for c in range(chunks):
        lanes = pl.ds(c * LANES, LANES)
        loads.append(pltpu.make_async_copy(f_hbm.at[:, :, :, lanes], fv.at[pl.ds(0, 4), c, own], load_sem.at[c, 1]))
    for copy in loads:
        copy.start()

    @pl.when(odd)
    def _():
        pl.semaphore_wait(barrier, len(greeted) + 2)
        for peer in (above, below):
            pl.semaphore_signal(ready_sem, inc=1, device_id={"col": peer}, device_id_type=MESH)

    @pl.when(jnp.logical_not(odd))
    def _():
        pl.semaphore_wait(barrier, len(greeted))

    def x_copy(n, source, target, peer):
        return pltpu.make_async_remote_copy(
            source, target, x_send.at[n], x_recv.at[n], device_id={"line": peer}, device_id_type=MESH)

    visc_copy = x_copy(0, v_hbm.at[last], x_left.at[4], right)
    visc_copy.start()
    x_copies = []
    for c in range(chunks):
        lanes = pl.ds(c * LANES, LANES)
        x_copies.append((
            x_copy(1 + c, f_hbm.at[:, last, :, lanes], x_left.at[pl.ds(0, 4), :, lanes], right),
            x_copy(1 + chunks + c, f_hbm.at[:, 0, :, lanes], x_right.at[:, :, lanes], left),
        ))
        for copy in x_copies[c]:
            copy.start()
    y_copies = []
    for c in range(chunks):
        lanes = pl.ds(c * LANES, LANES)
        y_copies.append([
            pltpu.make_async_remote_copy(
                source, target, y_send.at[side, c, n], y_recv.at[side, c, n],
                device_id={"col": peer}, device_id_type=MESH)
            for side, y, peer in ((0, 7, above), (1, 0, below))
            for n, source, target in (
                (0, f_hbm.at[:, :, y, lanes], halo_in.at[side, c, pl.ds(0, 4)]),
                (1, v_hbm.at[:, y, lanes], halo_in.at[side, c, 4]),
            )
        ])

    def start_y():
        for group in y_copies:
            for copy in group:
                copy.start()

    pl.when(odd)(start_y)
    for peer in column_peers:
        pl.semaphore_signal(plane_sem, inc=1, device_id={"line": peer}, device_id_type=MESH)

    for c in range(chunks):
        fv[4, c, 0] = jnp.zeros(shape, jnp.float32)
        fv[4, c, rows + 1] = jnp.zeros(shape, jnp.float32)

    for c in range(chunks):
        loads[c].wait()

    def matrix_row(c, q, k, a, h, e):
        r = 1.0 / (a + (h + e))
        m = a * r
        w = e * r
        rec[q, c, k] = r
        m_ref[c][q, k] = m
        w_ref[c][q, k] = w
        return m, w

    def matrix_step(i, carry):
        k = last - 1 - i
        new = []
        for c in range(chunks):
            total = fv[4, c, k + 1] + fv[4, c, k]
            for q in range(2):
                h, e, mass_right = carry[2 * c + q]
                m, w = matrix_row(c, q, k, rates(q) * total, h, e)
                new.append((1.0 + m * h, m * e, mass_right + w * h))
        return tuple(new)

    start = []
    for c in range(chunks):
        total = fv[4, c, rows] + fv[4, c, rows - 1]
        for q in range(2):
            a = rates(q) * total
            start.append((jnp.ones_like(a), a, jnp.zeros_like(a)))
    state = lax.fori_loop(0, last - 1, matrix_step, tuple(start))
    for c in range(chunks):
        for q in range(2):
            for n in range(3):
                mass[q, c, n] = state[2 * c + q][n]

    for c in range(chunks):
        loads[chunks + c].wait()
    lane = lax.broadcasted_iota(jnp.int32, shape, 1)
    level = lax.broadcasted_iota(jnp.int32, shape, 0)
    z_first, z_last = lane == 0, lane == LANES - 1
    y_first, y_last = level == 0, level == 7
    drift = 0.5 * ADVECTION
    half_next, half_prev = (jnp.where(wall, 0.0, 0.5 * CROSS_RATE) for wall in (y_last, y_first))
    inner_next, inner_prev = (jnp.where(wall, 0.0, drift) for wall in (y_last, y_first))

    flat = fv.reshape(5 * chunks * (rows + 2) * 8, LANES)

    half = 0.5 * CROSS_RATE

    def source_z(p):
        zero = jnp.zeros(shape, jnp.float32)

        def around(values):
            ahead = [pltpu.roll(x, LANES - 1, 1) for x in values] + [zero]
            behind = [zero] + [pltpu.roll(x, 1, 1) for x in values]
            z_next = [jnp.where(z_last, ahead[c + 1], ahead[c]) for c in range(chunks)]
            z_prev = [jnp.where(z_first, behind[c], behind[c + 1]) for c in range(chunks)]
            return z_next, z_prev

        visc = [half * fv[4, c, p] for c in range(chunks)]
        v_next, v_prev = around(visc)
        face_next = [visc[c] + v_next[c] for c in range(chunks)]
        face_prev = [visc[c] + v_prev[c] for c in range(chunks)]
        speed = [drift * fv[2, c, p] for c in range(chunks)]
        for q in range(2):
            ratio = (1.0, THERMAL_RATIO)[q]
            ahead, behind, centre = [], [], []
            for c in range(chunks):
                faces = [face_next[c], face_prev[c]] if q == 0 else [ratio * face_next[c], ratio * face_prev[c]]
                ahead.append(faces[0] - speed[c])
                behind.append(faces[1] + speed[c])
                centre.append(1.0 - (faces[0] + faces[1]))
            for a in ((0, 1, 2), (3,))[q]:
                own = [fv[a, c, p] for c in range(chunks)]
                z_next, z_prev = around(own)
                for c in range(chunks):
                    src[a, c, p - 1] = centre[c] * own[c] + (ahead[c] * z_next[c] + behind[c] * z_prev[c])

    def source_xy(p):
        for c in range(chunks):

            def level_pair(a):
                at = ((a * chunks + c) * (rows + 2) + p) * 8
                return flat[pl.ds(at + 1, 8), :], flat[pl.ds(at - 1, 8), :]

            v = fv[4, c, p]
            y_next, y_prev = level_pair(4)
            face_next = half_next * (v + y_next)
            face_prev = half_prev * (v + y_prev)
            own = [fv[a, c, p] for a in range(4)]
            speed_x = drift * own[0]
            speed_next, speed_prev = inner_next * own[1], inner_prev * own[1]
            for q in range(2):
                if q == 1:
                    face_next, face_prev = THERMAL_RATIO * face_next, THERMAL_RATIO * face_prev
                ahead, behind, both = face_next - speed_next, face_prev + speed_prev, face_next + face_prev
                for a in ((0, 1, 2), (3,))[q]:
                    y_next, y_prev = level_pair(a)
                    total = (ahead * y_next + behind * y_prev) - both * own[a]
                    total -= speed_x * (fv[a, c, p + 1] - fv[a, c, p - 1])
                    if a == 2:
                        total += BUOYANCY * own[3]
                    src[a, c, p - 1] += total

    def source_step(i, nothing):
        for n in range(TRIP):
            source_z(2 + TRIP * i + n)
        for n in range(TRIP):
            source_xy(2 + TRIP * i + n)
        return nothing

    trips = (rows - 2) // TRIP
    assert trips * TRIP == rows - 2

    @pl.when(jnp.logical_not(odd))
    def _():
        pl.semaphore_wait(ready_sem, 2)
        start_y()

    lax.fori_loop(0, EARLY, source_step, 0)

    visc_copy.wait_recv()
    inside_left = jnp.where(me == 0, 0.0, 1.0)
    inside_right = jnp.where(me == lines - 1, 0.0, 1.0)
    for c in range(chunks):
        total = fv[4, c, 1] + inside_left * x_left[4, :, pl.ds(c * LANES, LANES)]
        wall = (1.0 - inside_right) * fv[4, c, rows]
        for q in range(2):
            h, e, mass_right = (mass[q, c, n] for n in range(3))
            m, w = matrix_row(c, q, 0, rates(q) * total, h, e)
            mat_out[c, q, 0] = m * e
            mat_out[c, q, 1] = m * h
            mat_out[c, q, 2] = 1.0 + mass_right + w * h + rates(q) * wall

    pl.semaphore_wait(plane_sem, len(column_peers))

    def mat_copy(c, a):
        return pltpu.make_async_remote_copy(
            mat_out.at[c, a // 3], mat_in.at[me], mat_send.at[4 * c + a], mat_recv.at[me],
            device_id={"line": owner_of(c, a)}, device_id_type=MESH)

    slots = [(c, a) for c in range(chunks) for a in range(4)]
    for c, a in slots:

        @pl.when(me != owner_of(c, a))
        def _(c=c, a=a):
            mat_copy(c, a).start()

    mat_in[me] = mat_out[my_chunk, my_field // 3]

    lax.fori_loop(EARLY, trips, source_step, 0)
    source_z(1)
    source_z(rows)

    for c in range(chunks):
        for copy in x_copies[c]:
            copy.wait_recv()
        lanes = pl.ds(c * LANES, LANES)
        for a in range(4):
            fv[a, c, 0] = inside_left * x_left[a, :, lanes]
            fv[a, c, rows + 1] = inside_right * x_right[a, :, lanes]
    source_xy(1)
    source_xy(rows)

    edge = jnp.where(y_first | y_last, 0.5 * CROSS_RATE, 0.0)
    sign = jnp.where(y_last, -drift, jnp.where(y_first, drift, 0.0))

    def rhs_copy(c, a):
        return pltpu.make_async_remote_copy(
            rhs_out.at[4 * c + a], rhs_in.at[me], rhs_send.at[4 * c + a], rhs_recv.at[me],
            device_id={"line": owner_of(c, a)}, device_id_type=MESH)

    for c in range(chunks):
        for copy in y_copies[c]:
            copy.wait_recv()

        def finished(k):
            def beyond(a):
                low = jnp.broadcast_to(halo_in[0, c, a, pl.ds(k, 1), :], shape)
                high = jnp.broadcast_to(halo_in[1, c, a, pl.ds(k, 1), :], shape)
                return jnp.where(y_last, high, low)

            face = edge * (fv[4, c, k + 1] + beyond(4))
            speed = sign * fv[1, c, k + 1]
            faces = (face, THERMAL_RATIO * face)
            weights = (faces[0] + speed, faces[1] + speed)
            out = []
            for a in range(4):
                q = a // 3
                out.append(src[a, c, k] + (weights[q] * beyond(a) - faces[q] * fv[a, c, k + 1]))
            return out

        def rhs_row(k, carry):
            given = finished(k)
            new = []
            for a in range(4):
                q = a // 3
                passed, gathered = carry[a]
                d = given[a] + passed
                y_ref[c][a, k] = rec[q, c, k] * d
                new.append((m_ref[c][q, k] * d, gathered + w_ref[c][q, k] * d))
            return tuple(new)

        at_last = finished(last)
        zero = jnp.zeros(shape, jnp.float32)
        ends = tuple((zero, at_last[a]) for a in range(4))
        for k in range(last - 1, -1, -1):
            ends = rhs_row(k, ends)
        for a in range(4):
            rhs_out[4 * c + a, 0] = ends[a][0]
            rhs_out[4 * c + a, 1] = ends[a][1]

        for a in range(4):

            @pl.when(me != owner_of(c, a))
            def _(c=c, a=a):
                rhs_copy(c, a).start()

    rhs_in[me] = rhs_out[my_slot]

    def arrival(source, target, recv, j):
        return pltpu.make_async_remote_copy(
            source, target.at[j], rhs_send.at[0], recv.at[j], device_id={"line": left}, device_id_type=MESH)

    def mat_wait(d, nothing):
        arrival(mat_out.at[0, 0], mat_in, mat_recv, lax.rem(me + d, lines)).wait_recv()
        return nothing

    lax.fori_loop(1, lines, mat_wait, 0)

    def pivot_step(j, before):
        e = mat_in[j, 0]
        r = 1.0 / (e + before)
        m = e * r
        pivots[j, 0] = r
        pivots[j, 1] = m
        ahead = jnp.minimum(j + 1, lines - 1)
        own_mass = mat_in[j, 2] + jnp.where(j + 1 < lines, 1.0, 0.0) * mat_in[ahead, 1]
        return own_mass + m * before

    first = mat_in[0, 0] + (mat_in[0, 2] + mat_in[1, 1])
    final = lax.fori_loop(1, lines, pivot_step, first)
    final = 1.0 / final

    def rhs_wait(d, nothing):
        arrival(rhs_out.at[0], rhs_in, rhs_recv, lax.rem(me + d, lines)).wait_recv()
        return nothing

    lax.fori_loop(1, lines, rhs_wait, 0)
    given = [rhs_in[j, 1] + rhs_in[j + 1, 0] if j + 1 < lines else rhs_in[j, 1] for j in range(lines)]
    for j in range(1, lines):
        given[j] = given[j] + pivots[j, 1] * given[j - 1]
    value = final * given[lines - 1]
    sep[0] = jnp.zeros(shape, jnp.float32)
    sep[lines] = value
    for j in range(lines - 1, 0, -1):
        value = pivots[j, 0] * given[j - 1] + pivots[j, 1] * value
        sep[j] = value

    def sep_copy(j):
        return pltpu.make_async_remote_copy(
            sep.at[pl.ds(j, 2)], bounds.at[my_slot], sep_send.at[j], sep_recv.at[my_slot],
            device_id={"line": j}, device_id_type=MESH)

    for j in range(lines):

        @pl.when(me != j)
        def _(j=j):
            sep_copy(j).start()

    bounds[my_slot] = sep[pl.ds(me, 2)]

    visc_copy.wait_send()
    for group in x_copies + y_copies:
        for copy in group:
            copy.wait_send()
    for c, a in slots:

        @pl.when(me != owner_of(c, a))
        def _(c=c, a=a):
            mat_copy(c, a).wait_send()
            rhs_copy(c, a).wait_send()

    for c in range(chunks):
        for a in range(4):

            @pl.when(me != owner_of(c, a))
            def _(c=c, a=a):
                arrival(sep.at[pl.ds(0, 2)], bounds, sep_recv, 4 * c + a).wait_recv()

        if c < chunks - 1:
            substitute(
                last, y_ref[c], m_ref[c], w_ref[c],
                [(bounds[4 * c + a, 0], bounds[4 * c + a, 1]) for a in range(4)], u_out.at[c])
        else:
            for a in range(4):
                b_out[a] = bounds[4 * c + a]

    for j in range(lines):

        @pl.when(me != j)
        def _(j=j):
            sep_copy(j).wait_send()


def substitute(last, y, m, w, ends, out):
    def row(k, before):
        new = []
        for a in range(4):
            q = a // 3
            u = (y[a, k] + w[q, k] * ends[a][1]) + m[q, k] * before[a]
            out[a, k] = u
            new.append(u)
        return tuple(new)

    def step(i, before):
        for n in range(STEP):
            before = row(1 + STEP * i + n, before)
        return before

    assert (last - 1) % STEP == 0
    first = row(0, tuple(end[0] for end in ends))
    lax.fori_loop(0, (last - 1) // STEP, step, first)
    for a in range(4):
        out[a, last] = ends[a][1]


def back_kernel(rows, chunks, u, y, m, w, b, out, buf, sem):
    copies = []

    def write(c, source):
        copy = pltpu.make_async_copy(source, out.at[:, :, :, pl.ds(c * LANES, LANES)], sem.at[c])
        copy.start()
        copies.append(copy)

    for c in range(chunks - 1):
        write(c, u.at[c])
    substitute(rows - 1, y, m, w, [(b[a, 0], b[a, 1]) for a in range(4)], buf)
    write(chunks - 1, buf)
    for copy in copies:
        copy.wait()


def in_place(array):
    return pltpu.with_memory_space_constraint(array, pltpu.HBM)


def solution(mesh):
    lines, cols = mesh.shape["line"], mesh.shape["col"]

    def local(fields, viscosity):
        _, rows, deep, wide = fields.shape
        chunks = wide // LANES
        assert deep == 8 and 4 * chunks == lines
        f32 = jnp.float32
        tile = (8, LANES)
        vmem = pl.BlockSpec(memory_space=pltpu.VMEM)
        anywhere = pl.BlockSpec(memory_space=pl.ANY)
        dma = pltpu.SemaphoreType.DMA
        parts = pl.pallas_call(
            functools.partial(main_kernel, lines, cols, rows, chunks),
            out_shape=(
                jax.ShapeDtypeStruct((chunks - 1, 4, rows) + tile, f32),
                jax.ShapeDtypeStruct((4, rows) + tile, f32),
                jax.ShapeDtypeStruct((2, rows) + tile, f32),
                jax.ShapeDtypeStruct((2, rows) + tile, f32),
                jax.ShapeDtypeStruct((4, 2) + tile, f32),
            ),
            in_specs=[anywhere, anywhere],
            out_specs=(vmem,) * 5,
            scratch_shapes=[
                pltpu.VMEM((5, chunks, rows + 2) + tile, f32),
                pltpu.VMEM((4, chunks, rows) + tile, f32),
                pltpu.VMEM((chunks - 1, 4, rows) + tile, f32),
                pltpu.VMEM((chunks - 1, 2, rows) + tile, f32),
                pltpu.VMEM((chunks - 1, 2, rows) + tile, f32),
                pltpu.VMEM((2, chunks, rows) + tile, f32),
                pltpu.VMEM((2, chunks, 3) + tile, f32),
                pltpu.VMEM((5, deep, wide), f32),
                pltpu.VMEM((4, deep, wide), f32),
                pltpu.VMEM((2, chunks, 5, rows, LANES), f32),
                pltpu.VMEM((chunks, 2, 3) + tile, f32),
                pltpu.VMEM((lines, 3) + tile, f32),
                pltpu.VMEM((lines, 2) + tile, f32),
                pltpu.VMEM((lines, 2) + tile, f32),
                pltpu.VMEM((lines + 1,) + tile, f32),
                pltpu.VMEM((lines, 2) + tile, f32),
                pltpu.VMEM((lines, 2) + tile, f32),
                dma((chunks, 2)),
                dma((1 + 2 * chunks,)), dma((1 + 2 * chunks,)), dma((2, chunks, 2)), dma((2, chunks, 2)),
                dma((lines,)), dma((lines,)), dma((lines,)), dma((lines,)), dma((lines,)), dma((lines,)),
                pltpu.SemaphoreType.REGULAR, pltpu.SemaphoreType.REGULAR,
            ],
            compiler_params=pltpu.CompilerParams(
                collective_id=0, has_side_effects=True, vmem_limit_bytes=40 << 20
            ),
            name="eliminate",
        )(in_place(fields), in_place(viscosity))
        return pl.pallas_call(
            functools.partial(back_kernel, rows, chunks),
            out_shape=jax.ShapeDtypeStruct((4, rows, 8, wide), f32),
            in_specs=[vmem] * 5,
            out_specs=anywhere,
            scratch_shapes=[pltpu.VMEM((4, rows) + tile, f32), dma((chunks,))],
            compiler_params=pltpu.CompilerParams(vmem_limit_bytes=24 << 20),
            name="substitute",
        )(*parts)

    return jax.shard_map(
        local,
        mesh=mesh,
        in_specs=(P(None, "line", "col", None), P("line", "col", None)),
        out_specs=P(None, "line", "col", None),
        check_vma=False,
    )
```

```python
import functools

import jax
import jax.numpy as jnp
from jax import lax
from jax.experimental import pallas as pl
from jax.experimental.pallas import tpu as pltpu
from jax.sharding import PartitionSpec as P

STIFF = 3072.0
THERMAL_RATIO = 0.8
CROSS_RATE = 0.2
ADVECTION = 0.25
BUOYANCY = 2.0
MESH = pl.DeviceIdType.MESH
LANES = 128
STEP = 15
TRIP = 5
EARLY = 2
SIDE = 4


def rates(q):
    return 0.5 * STIFF * (1.0 if q == 0 else THERMAL_RATIO)


def owner_of(c, a):
    near_x, near_y, high_x, high_y = c % 2, c // 2, a % 2, a // 2
    x = (2 + near_x) if high_x else (1 - near_x)
    y = (2 + near_y) if high_y else (1 - near_y)
    return y * SIDE + x


def slot_of(me):
    x, y = lax.rem(me, SIDE), me // SIDE
    high_x, high_y = x // 2, y // 2
    near_x = jnp.where(high_x == 1, x - 2, 1 - x)
    near_y = jnp.where(high_y == 1, y - 2, 1 - y)
    return near_x + 2 * near_y, high_x + 2 * high_y


def main_kernel(
    lines, cols, rows, chunks,
    f_hbm, v_hbm,
    u_out, y_end, m_end, w_end, b_out,
    fv, src, y_all, m_all, w_all, rec, mass, x_left, x_right, halo_out, halo_in,
    mat_out, mat_in, rhs_out, rhs_in, sep, bounds, pivots,
    load_sem, x_send, x_recv, y_send, y_recv,
    mat_send, mat_recv, rhs_send, rhs_recv, sep_send, sep_recv, plane_sem, ready_sem,
):
    me = lax.axis_index("line")
    col = lax.axis_index("col")
    right, left = lax.rem(me + 1, lines), lax.rem(me + lines - 1, lines)
    above, below = lax.rem(col + 1, cols), lax.rem(col + cols - 1, cols)
    row_of, place = me // SIDE, lax.rem(me, SIDE)
    my_chunk, my_field = slot_of(me)
    my_slot = 4 * my_chunk + my_field
    last = rows - 1
    shape = (8, LANES)
    y_ref = [y_all.at[c] for c in range(chunks - 1)] + [y_end]
    m_ref = [m_all.at[c] for c in range(chunks - 1)] + [m_end]
    w_ref = [w_all.at[c] for c in range(chunks - 1)] + [w_end]

    barrier = pltpu.get_barrier_semaphore()
    row_peers = [row_of * SIDE + lax.rem(place + d, SIDE) for d in range(1, SIDE)]
    column_peers = [lax.rem(row_of + d, lines // SIDE) * SIDE + place for d in range(1, lines // SIDE)]
    greeted = [{"line": p} for p in [right, left] + row_peers + column_peers]
    for peer in greeted:
        pl.semaphore_signal(barrier, inc=1, device_id=peer, device_id_type=MESH)
    odd = lax.rem(col, 2) == 1

    @pl.when(jnp.logical_not(odd))
    def _():
        for peer in (above, below):
            pl.semaphore_signal(barrier, inc=1, device_id={"col": peer}, device_id_type=MESH)

    loads = []
    own = pl.ds(1, rows)
    for c in range(chunks):
        lanes = pl.ds(c * LANES, LANES)
        loads.append(pltpu.make_async_copy(v_hbm.at[:, :, lanes], fv.at[4, c, own], load_sem.at[c, 0]))
    for c in range(chunks):
        lanes = pl.ds(c * LANES, LANES)
        loads.append(pltpu.make_async_copy(f_hbm.at[:, :, :, lanes], fv.at[pl.ds(0, 4), c, own], load_sem.at[c, 1]))
    for c in range(chunks):
        loads[c].start()
        loads[chunks + c].start()

    @pl.when(odd)
    def _():
        pl.semaphore_wait(barrier, len(greeted) + 2)
        for peer in (above, below):
            pl.semaphore_signal(ready_sem, inc=1, device_id={"col": peer}, device_id_type=MESH)

    @pl.when(jnp.logical_not(odd))
    def _():
        pl.semaphore_wait(barrier, len(greeted))

    def x_copy(n, source, target, peer):
        return pltpu.make_async_remote_copy(
            source, target, x_send.at[n], x_recv.at[n], device_id={"line": peer}, device_id_type=MESH)

    visc_copy = x_copy(0, v_hbm.at[last], x_left.at[4], right)
    visc_copy.start()
    x_copies = []
    for c in range(chunks):
        lanes = pl.ds(c * LANES, LANES)
        x_copies.append((
            x_copy(1 + c, f_hbm.at[:, last, :, lanes], x_left.at[pl.ds(0, 4), :, lanes], right),
            x_copy(1 + chunks + c, f_hbm.at[:, 0, :, lanes], x_right.at[:, :, lanes], left),
        ))
        for copy in x_copies[c]:
            copy.start()
    y_copies = []
    for c in range(chunks):
        y_copies.append([
            pltpu.make_async_remote_copy(
                halo_out.at[side, c], halo_in.at[side, c], y_send.at[side, c], y_recv.at[side, c],
                device_id={"col": peer}, device_id_type=MESH)
            for side, peer in ((0, above), (1, below))
        ])

    def start_y():
        for group in y_copies:
            for copy in group:
                copy.start()

    for peer in column_peers:
        pl.semaphore_signal(plane_sem, inc=1, device_id={"line": peer}, device_id_type=MESH)

    for c in range(chunks):
        fv[4, c, 0] = jnp.zeros(shape, jnp.float32)
        fv[4, c, rows + 1] = jnp.zeros(shape, jnp.float32)

    flat = fv.reshape(5 * chunks * (rows + 2) * 8, LANES)
    for c in range(chunks):
        loads[c].wait()
        loads[chunks + c].wait()
        for a in range(5):
            for side, y in ((0, 7), (1, 0)):
                for g in range(0, rows, 8):
                    at = ((a * chunks + c) * (rows + 2) + 1 + g) * 8 + y
                    halo_out[side, c, a, g : g + 8, :] = flat[pl.ds(at, 8, stride=8), :]
    pl.when(odd)(start_y)

    def matrix_row(c, q, k, a, h, e):
        r = 1.0 / (a + (h + e))
        m = a * r
        w = e * r
        rec[q, c, k] = r
        m_ref[c][q, k] = m
        w_ref[c][q, k] = w
        return m, w

    def matrix_step(i, carry):
        k = last - 1 - i
        new = []
        for c in range(chunks):
            total = fv[4, c, k + 1] + fv[4, c, k]
            for q in range(2):
                h, e, mass_right = carry[2 * c + q]
                m, w = matrix_row(c, q, k, rates(q) * total, h, e)
                new.append((1.0 + m * h, m * e, mass_right + w * h))
        return tuple(new)

    start = []
    for c in range(chunks):
        total = fv[4, c, rows] + fv[4, c, rows - 1]
        for q in range(2):
            a = rates(q) * total
            start.append((jnp.ones_like(a), a, jnp.zeros_like(a)))
    state = lax.fori_loop(0, last - 1, matrix_step, tuple(start))
    for c in range(chunks):
        for q in range(2):
            for n in range(3):
                mass[q, c, n] = state[2 * c + q][n]

    lane = lax.broadcasted_iota(jnp.int32, shape, 1)
    level = lax.broadcasted_iota(jnp.int32, shape, 0)
    z_first, z_last = lane == 0, lane == LANES - 1
    y_first, y_last = level == 0, level == 7
    drift = 0.5 * ADVECTION
    half_next, half_prev = (jnp.where(wall, 0.0, 0.5 * CROSS_RATE) for wall in (y_last, y_first))
    inner_next, inner_prev = (jnp.where(wall, 0.0, drift) for wall in (y_last, y_first))

    half = 0.5 * CROSS_RATE

    def source_z(p):
        zero = jnp.zeros(shape, jnp.float32)

        def around(values):
            ahead = [pltpu.roll(x, LANES - 1, 1) for x in values] + [zero]
            behind = [zero] + [pltpu.roll(x, 1, 1) for x in values]
            z_next = [jnp.where(z_last, ahead[c + 1], ahead[c]) for c in range(chunks)]
            z_prev = [jnp.where(z_first, behind[c], behind[c + 1]) for c in range(chunks)]
            return z_next, z_prev

        visc = [half * fv[4, c, p] for c in range(chunks)]
        v_next, v_prev = around(visc)
        face_next = [visc[c] + v_next[c] for c in range(chunks)]
        face_prev = [visc[c] + v_prev[c] for c in range(chunks)]
        speed = [drift * fv[2, c, p] for c in range(chunks)]
        for q in range(2):
            ratio = (1.0, THERMAL_RATIO)[q]
            ahead, behind, centre = [], [], []
            for c in range(chunks):
                faces = [face_next[c], face_prev[c]] if q == 0 else [ratio * face_next[c], ratio * face_prev[c]]
                ahead.append(faces[0] - speed[c])
                behind.append(faces[1] + speed[c])
                centre.append(1.0 - (faces[0] + faces[1]))
            for a in ((0, 1, 2), (3,))[q]:
                own = [fv[a, c, p] for c in range(chunks)]
                z_next, z_prev = around(own)
                for c in range(chunks):
                    src[a, c, p - 1] = centre[c] * own[c] + (ahead[c] * z_next[c] + behind[c] * z_prev[c])

    def source_xy(p):
        for c in range(chunks):

            def level_pair(a):
                at = ((a * chunks + c) * (rows + 2) + p) * 8
                return flat[pl.ds(at + 1, 8), :], flat[pl.ds(at - 1, 8), :]

            v = fv[4, c, p]
            y_next, y_prev = level_pair(4)
            face_next = half_next * (v + y_next)
            face_prev = half_prev * (v + y_prev)
            own = [fv[a, c, p] for a in range(4)]
            speed_x = drift * own[0]
            speed_next, speed_prev = inner_next * own[1], inner_prev * own[1]
            for q in range(2):
                if q == 1:
                    face_next, face_prev = THERMAL_RATIO * face_next, THERMAL_RATIO * face_prev
                ahead, behind, both = face_next - speed_next, face_prev + speed_prev, face_next + face_prev
                for a in ((0, 1, 2), (3,))[q]:
                    y_next, y_prev = level_pair(a)
                    total = (ahead * y_next + behind * y_prev) - both * own[a]
                    total -= speed_x * (fv[a, c, p + 1] - fv[a, c, p - 1])
                    if a == 2:
                        total += BUOYANCY * own[3]
                    src[a, c, p - 1] += total

    def source_step(i, nothing):
        for n in range(TRIP):
            source_z(2 + TRIP * i + n)
        for n in range(TRIP):
            source_xy(2 + TRIP * i + n)
        return nothing

    trips = (rows - 2) // TRIP
    assert trips * TRIP == rows - 2

    @pl.when(jnp.logical_not(odd))
    def _():
        pl.semaphore_wait(ready_sem, 2)
        start_y()

    lax.fori_loop(0, EARLY, source_step, 0)

    visc_copy.wait_recv()
    inside_left = jnp.where(me == 0, 0.0, 1.0)
    inside_right = jnp.where(me == lines - 1, 0.0, 1.0)
    for c in range(chunks):
        total = fv[4, c, 1] + inside_left * x_left[4, :, pl.ds(c * LANES, LANES)]
        wall = (1.0 - inside_right) * fv[4, c, rows]
        for q in range(2):
            h, e, mass_right = (mass[q, c, n] for n in range(3))
            m, w = matrix_row(c, q, 0, rates(q) * total, h, e)
            mat_out[c, q, 0] = m * e
            mat_out[c, q, 1] = m * h
            mat_out[c, q, 2] = 1.0 + mass_right + w * h + rates(q) * wall

    pl.semaphore_wait(plane_sem, len(column_peers))

    def mat_copy(c, a):
        return pltpu.make_async_remote_copy(
            mat_out.at[c, a // 3], mat_in.at[me], mat_send.at[4 * c + a], mat_recv.at[me],
            device_id={"line": owner_of(c, a)}, device_id_type=MESH)

    slots = [(c, a) for c in range(chunks) for a in range(4)]
    for c, a in slots:

        @pl.when(me != owner_of(c, a))
        def _(c=c, a=a):
            mat_copy(c, a).start()

    mat_in[me] = mat_out[my_chunk, my_field // 3]

    lax.fori_loop(EARLY, trips, source_step, 0)
    source_z(1)
    source_z(rows)

    for c in range(chunks):
        for copy in x_copies[c]:
            copy.wait_recv()
        lanes = pl.ds(c * LANES, LANES)
        for a in range(4):
            fv[a, c, 0] = inside_left * x_left[a, :, lanes]
            fv[a, c, rows + 1] = inside_right * x_right[a, :, lanes]
    source_xy(1)
    source_xy(rows)

    edge = jnp.where(y_first | y_last, 0.5 * CROSS_RATE, 0.0)
    sign = jnp.where(y_last, -drift, jnp.where(y_first, drift, 0.0))

    def rhs_copy(c, a):
        return pltpu.make_async_remote_copy(
            rhs_out.at[4 * c + a], rhs_in.at[me], rhs_send.at[4 * c + a], rhs_recv.at[me],
            device_id={"line": owner_of(c, a)}, device_id_type=MESH)

    for c in range(chunks):
        for copy in y_copies[c]:
            copy.wait_recv()

        def finished(k):
            def beyond(a):
                low = jnp.broadcast_to(halo_in[0, c, a, pl.ds(k, 1), :], shape)
                high = jnp.broadcast_to(halo_in[1, c, a, pl.ds(k, 1), :], shape)
                return jnp.where(y_last, high, low)

            face = edge * (fv[4, c, k + 1] + beyond(4))
            speed = sign * fv[1, c, k + 1]
            faces = (face, THERMAL_RATIO * face)
            weights = (faces[0] + speed, faces[1] + speed)
            out = []
            for a in range(4):
                q = a // 3
                out.append(src[a, c, k] + (weights[q] * beyond(a) - faces[q] * fv[a, c, k + 1]))
            return out

        def rhs_row(k, carry):
            given = finished(k)
            new = []
            for a in range(4):
                q = a // 3
                passed, gathered = carry[a]
                d = given[a] + passed
                y_ref[c][a, k] = rec[q, c, k] * d
                new.append((m_ref[c][q, k] * d, gathered + w_ref[c][q, k] * d))
            return tuple(new)

        at_last = finished(last)
        zero = jnp.zeros(shape, jnp.float32)
        ends = tuple((zero, at_last[a]) for a in range(4))
        for k in range(last - 1, -1, -1):
            ends = rhs_row(k, ends)
        for a in range(4):
            rhs_out[4 * c + a, 0] = ends[a][0]
            rhs_out[4 * c + a, 1] = ends[a][1]

        for a in range(4):

            @pl.when(me != owner_of(c, a))
            def _(c=c, a=a):
                rhs_copy(c, a).start()

    rhs_in[me] = rhs_out[my_slot]

    def arrival(source, target, recv, j):
        return pltpu.make_async_remote_copy(
            source, target.at[j], rhs_send.at[0], recv.at[j], device_id={"line": left}, device_id_type=MESH)

    def mat_wait(d, nothing):
        arrival(mat_out.at[0, 0], mat_in, mat_recv, lax.rem(me + d, lines)).wait_recv()
        return nothing

    lax.fori_loop(1, lines, mat_wait, 0)

    def pivot_step(j, before):
        e = mat_in[j, 0]
        r = 1.0 / (e + before)
        m = e * r
        pivots[j, 0] = r
        pivots[j, 1] = m
        ahead = jnp.minimum(j + 1, lines - 1)
        own_mass = mat_in[j, 2] + jnp.where(j + 1 < lines, 1.0, 0.0) * mat_in[ahead, 1]
        return own_mass + m * before

    first = mat_in[0, 0] + (mat_in[0, 2] + mat_in[1, 1])
    final = lax.fori_loop(1, lines, pivot_step, first)
    final = 1.0 / final

    def rhs_wait(d, nothing):
        arrival(rhs_out.at[0], rhs_in, rhs_recv, lax.rem(me + d, lines)).wait_recv()
        return nothing

    lax.fori_loop(1, lines, rhs_wait, 0)
    given = [rhs_in[j, 1] + rhs_in[j + 1, 0] if j + 1 < lines else rhs_in[j, 1] for j in range(lines)]
    for j in range(1, lines):
        given[j] = given[j] + pivots[j, 1] * given[j - 1]
    value = final * given[lines - 1]
    sep[0] = jnp.zeros(shape, jnp.float32)
    sep[lines] = value
    for j in range(lines - 1, 0, -1):
        value = pivots[j, 0] * given[j - 1] + pivots[j, 1] * value
        sep[j] = value

    def sep_copy(j):
        return pltpu.make_async_remote_copy(
            sep.at[pl.ds(j, 2)], bounds.at[my_slot], sep_send.at[j], sep_recv.at[my_slot],
            device_id={"line": j}, device_id_type=MESH)

    for j in range(lines):

        @pl.when(me != j)
        def _(j=j):
            sep_copy(j).start()

    bounds[my_slot] = sep[pl.ds(me, 2)]

    visc_copy.wait_send()
    for group in x_copies + y_copies:
        for copy in group:
            copy.wait_send()
    for c, a in slots:

        @pl.when(me != owner_of(c, a))
        def _(c=c, a=a):
            mat_copy(c, a).wait_send()
            rhs_copy(c, a).wait_send()

    for c in range(chunks):
        for a in range(4):

            @pl.when(me != owner_of(c, a))
            def _(c=c, a=a):
                arrival(sep.at[pl.ds(0, 2)], bounds, sep_recv, 4 * c + a).wait_recv()

        if c < chunks - 1:
            substitute(
                last, y_ref[c], m_ref[c], w_ref[c],
                [(bounds[4 * c + a, 0], bounds[4 * c + a, 1]) for a in range(4)], u_out.at[c])
        else:
            for a in range(4):
                b_out[a] = bounds[4 * c + a]

    for j in range(lines):

        @pl.when(me != j)
        def _(j=j):
            sep_copy(j).wait_send()


def substitute(last, y, m, w, ends, out):
    def row(k, before):
        new = []
        for a in range(4):
            q = a // 3
            u = (y[a, k] + w[q, k] * ends[a][1]) + m[q, k] * before[a]
            out[a, k] = u
            new.append(u)
        return tuple(new)

    def step(i, before):
        for n in range(STEP):
            before = row(1 + STEP * i + n, before)
        return before

    assert (last - 1) % STEP == 0
    first = row(0, tuple(end[0] for end in ends))
    lax.fori_loop(0, (last - 1) // STEP, step, first)
    for a in range(4):
        out[a, last] = ends[a][1]


def back_kernel(rows, chunks, u, y, m, w, b, out, buf, sem):
    copies = []

    def write(c, source):
        copy = pltpu.make_async_copy(source, out.at[:, :, :, pl.ds(c * LANES, LANES)], sem.at[c])
        copy.start()
        copies.append(copy)

    for c in range(chunks - 1):
        write(c, u.at[c])
    substitute(rows - 1, y, m, w, [(b[a, 0], b[a, 1]) for a in range(4)], buf)
    write(chunks - 1, buf)
    for copy in copies:
        copy.wait()


def in_place(array):
    return pltpu.with_memory_space_constraint(array, pltpu.HBM)


def solution(mesh):
    lines, cols = mesh.shape["line"], mesh.shape["col"]

    def local(fields, viscosity):
        _, rows, deep, wide = fields.shape
        chunks = wide // LANES
        assert deep == 8 and 4 * chunks == lines
        f32 = jnp.float32
        tile = (8, LANES)
        vmem = pl.BlockSpec(memory_space=pltpu.VMEM)
        anywhere = pl.BlockSpec(memory_space=pl.ANY)
        dma = pltpu.SemaphoreType.DMA
        parts = pl.pallas_call(
            functools.partial(main_kernel, lines, cols, rows, chunks),
            out_shape=(
                jax.ShapeDtypeStruct((chunks - 1, 4, rows) + tile, f32),
                jax.ShapeDtypeStruct((4, rows) + tile, f32),
                jax.ShapeDtypeStruct((2, rows) + tile, f32),
                jax.ShapeDtypeStruct((2, rows) + tile, f32),
                jax.ShapeDtypeStruct((4, 2) + tile, f32),
            ),
            in_specs=[anywhere, anywhere],
            out_specs=(vmem,) * 5,
            scratch_shapes=[
                pltpu.VMEM((5, chunks, rows + 2) + tile, f32),
                pltpu.VMEM((4, chunks, rows) + tile, f32),
                pltpu.VMEM((chunks - 1, 4, rows) + tile, f32),
                pltpu.VMEM((chunks - 1, 2, rows) + tile, f32),
                pltpu.VMEM((chunks - 1, 2, rows) + tile, f32),
                pltpu.VMEM((2, chunks, rows) + tile, f32),
                pltpu.VMEM((2, chunks, 3) + tile, f32),
                pltpu.VMEM((5, deep, wide), f32),
                pltpu.VMEM((4, deep, wide), f32),
                pltpu.VMEM((2, chunks, 5, rows, LANES), f32),
                pltpu.VMEM((2, chunks, 5, rows, LANES), f32),
                pltpu.VMEM((chunks, 2, 3) + tile, f32),
                pltpu.VMEM((lines, 3) + tile, f32),
                pltpu.VMEM((lines, 2) + tile, f32),
                pltpu.VMEM((lines, 2) + tile, f32),
                pltpu.VMEM((lines + 1,) + tile, f32),
                pltpu.VMEM((lines, 2) + tile, f32),
                pltpu.VMEM((lines, 2) + tile, f32),
                dma((chunks, 2)),
                dma((1 + 2 * chunks,)), dma((1 + 2 * chunks,)), dma((2, chunks)), dma((2, chunks)),
                dma((lines,)), dma((lines,)), dma((lines,)), dma((lines,)), dma((lines,)), dma((lines,)),
                pltpu.SemaphoreType.REGULAR, pltpu.SemaphoreType.REGULAR,
            ],
            compiler_params=pltpu.CompilerParams(
                collective_id=0, has_side_effects=True, vmem_limit_bytes=40 << 20
            ),
            name="eliminate",
        )(in_place(fields), in_place(viscosity))
        return pl.pallas_call(
            functools.partial(back_kernel, rows, chunks),
            out_shape=jax.ShapeDtypeStruct((4, rows, 8, wide), f32),
            in_specs=[vmem] * 5,
            out_specs=anywhere,
            scratch_shapes=[pltpu.VMEM((4, rows) + tile, f32), dma((chunks,))],
            compiler_params=pltpu.CompilerParams(vmem_limit_bytes=24 << 20),
            name="substitute",
        )(*parts)

    return jax.shard_map(
        local,
        mesh=mesh,
        in_specs=(P(None, "line", "col", None), P("line", "col", None)),
        out_specs=P(None, "line", "col", None),
        check_vma=False,
    )
```

```python
import functools

import jax
import jax.numpy as jnp
from jax import lax
from jax.experimental import pallas as pl
from jax.experimental.pallas import tpu as pltpu
from jax.sharding import PartitionSpec as P

STIFF = 3072.0
THERMAL_RATIO = 0.8
CROSS_RATE = 0.2
ADVECTION = 0.25
BUOYANCY = 2.0
MESH = pl.DeviceIdType.MESH
LANES = 128
STEP = 15
TRIP = 5
EARLY = 2
SWAP = {2: 15, 15: 2}
SIDE = 4


def rates(q):
    return 0.5 * STIFF * (1.0 if q == 0 else THERMAL_RATIO)


def owner_of(c, a):
    near_x, near_y, high_x, high_y = c % 2, c // 2, a % 2, a // 2
    x = (2 + near_x) if high_x else (1 - near_x)
    y = (2 + near_y) if high_y else (1 - near_y)
    return SWAP.get(y * SIDE + x, y * SIDE + x)


def slot_of(me):
    for one, other in SWAP.items():
        if one < other:
            me = jnp.where(me == one, other, jnp.where(me == other, one, me))
    x, y = lax.rem(me, SIDE), me // SIDE
    high_x, high_y = x // 2, y // 2
    near_x = jnp.where(high_x == 1, x - 2, 1 - x)
    near_y = jnp.where(high_y == 1, y - 2, 1 - y)
    return near_x + 2 * near_y, high_x + 2 * high_y


def main_kernel(
    lines, cols, rows, chunks,
    f_hbm, v_hbm,
    u_out, y_end, m_end, w_end, b_out,
    fv, src, y_all, m_all, w_all, rec, mass, x_left, x_right, halo_out, halo_in,
    mat_out, mat_in, rhs_out, rhs_in, sep, bounds, pivots,
    load_sem, x_send, x_recv, y_send, y_recv,
    mat_send, mat_recv, rhs_send, rhs_recv, sep_send, sep_recv, plane_sem, ready_sem,
):
    me = lax.axis_index("line")
    col = lax.axis_index("col")
    right, left = lax.rem(me + 1, lines), lax.rem(me + lines - 1, lines)
    above, below = lax.rem(col + 1, cols), lax.rem(col + cols - 1, cols)
    row_of, place = me // SIDE, lax.rem(me, SIDE)
    my_chunk, my_field = slot_of(me)
    my_slot = 4 * my_chunk + my_field
    last = rows - 1
    shape = (8, LANES)
    y_ref = [y_all.at[c] for c in range(chunks - 1)] + [y_end]
    m_ref = [m_all.at[c] for c in range(chunks - 1)] + [m_end]
    w_ref = [w_all.at[c] for c in range(chunks - 1)] + [w_end]

    barrier = pltpu.get_barrier_semaphore()
    row_peers = [row_of * SIDE + lax.rem(place + d, SIDE) for d in range(1, SIDE)]
    column_peers = [lax.rem(row_of + d, lines // SIDE) * SIDE + place for d in range(1, lines // SIDE)]
    greeted = [{"line": p} for p in [right, left] + row_peers + column_peers]
    for peer in greeted:
        pl.semaphore_signal(barrier, inc=1, device_id=peer, device_id_type=MESH)
    odd = lax.rem(col, 2) == 1

    @pl.when(jnp.logical_not(odd))
    def _():
        for peer in (above, below):
            pl.semaphore_signal(barrier, inc=1, device_id={"col": peer}, device_id_type=MESH)

    loads = []
    own = pl.ds(1, rows)
    for c in range(chunks):
        lanes = pl.ds(c * LANES, LANES)
        loads.append(pltpu.make_async_copy(v_hbm.at[:, :, lanes], fv.at[4, c, own], load_sem.at[c, 0]))
    for c in range(chunks):
        lanes = pl.ds(c * LANES, LANES)
        loads.append(pltpu.make_async_copy(f_hbm.at[:, :, :, lanes], fv.at[pl.ds(0, 4), c, own], load_sem.at[c, 1]))
    for c in range(chunks):
        loads[c].start(priority=1 if c == 0 else 0)
        loads[chunks + c].start(priority=1 if c == 0 else 0)

    @pl.when(odd)
    def _():
        pl.semaphore_wait(barrier, len(greeted) + 2)
        for side, peer in ((1, above), (0, below)):
            pl.semaphore_signal(ready_sem.at[side], inc=1, device_id={"col": peer}, device_id_type=MESH)

    @pl.when(jnp.logical_not(odd))
    def _():
        pl.semaphore_wait(barrier, len(greeted))

    def x_copy(n, source, target, peer):
        return pltpu.make_async_remote_copy(
            source, target, x_send.at[n], x_recv.at[n], device_id={"line": peer}, device_id_type=MESH)

    visc_copy = x_copy(0, v_hbm.at[last], x_left.at[4], right)
    visc_copy.start()
    x_copies = []
    for c in range(chunks):
        lanes = pl.ds(c * LANES, LANES)
        x_copies.append((
            x_copy(1 + c, f_hbm.at[:, last, :, lanes], x_left.at[pl.ds(0, 4), :, lanes], right),
            x_copy(1 + chunks + c, f_hbm.at[:, 0, :, lanes], x_right.at[:, :, lanes], left),
        ))
        for copy in x_copies[c]:
            copy.start()
    y_copies = []
    for c in range(chunks):
        y_copies.append([
            pltpu.make_async_remote_copy(
                halo_out.at[side, c], halo_in.at[side, c], y_send.at[side, c], y_recv.at[side, c],
                device_id={"col": peer}, device_id_type=MESH)
            for side, peer in ((0, above), (1, below))
        ])

    def start_when_in(side):
        pl.semaphore_wait(ready_sem.at[side], 1)
        for group in y_copies:
            group[side].start()

    even, lowest = jnp.logical_not(odd), col == 0

    for peer in column_peers:
        pl.semaphore_signal(plane_sem, inc=1, device_id={"line": peer}, device_id_type=MESH)

    for c in range(chunks):
        fv[4, c, 0] = jnp.zeros(shape, jnp.float32)
        fv[4, c, rows + 1] = jnp.zeros(shape, jnp.float32)

    flat = fv.reshape(5 * chunks * (rows + 2) * 8, LANES)
    for c in range(chunks):
        loads[c].wait()
        loads[chunks + c].wait()
        for a in range(5):
            for side, y in ((0, 7), (1, 0)):
                for g in range(0, rows, 8):
                    at = ((a * chunks + c) * (rows + 2) + 1 + g) * 8 + y
                    halo_out[side, c, a, g : g + 8, :] = flat[pl.ds(at, 8, stride=8), :]

        @pl.when(odd)
        def _(c=c):
            for copy in y_copies[c]:
                copy.start()
    pl.when(lowest)(lambda: start_when_in(0))
    pl.when(even & jnp.logical_not(lowest))(lambda: start_when_in(1))


    def matrix_row(c, q, k, a, h, e):
        r = 1.0 / (a + (h + e))
        m = a * r
        w = e * r
        rec[q, c, k] = r
        m_ref[c][q, k] = m
        w_ref[c][q, k] = w
        return m, w

    def matrix_step(i, carry):
        k = last - 1 - i
        new = []
        for c in range(chunks):
            total = fv[4, c, k + 1] + fv[4, c, k]
            for q in range(2):
                h, e, mass_right = carry[2 * c + q]
                m, w = matrix_row(c, q, k, rates(q) * total, h, e)
                new.append((1.0 + m * h, m * e, mass_right + w * h))
        return tuple(new)

    start = []
    for c in range(chunks):
        total = fv[4, c, rows] + fv[4, c, rows - 1]
        for q in range(2):
            a = rates(q) * total
            start.append((jnp.ones_like(a), a, jnp.zeros_like(a)))
    state = lax.fori_loop(0, last - 1, matrix_step, tuple(start))
    for c in range(chunks):
        for q in range(2):
            for n in range(3):
                mass[q, c, n] = state[2 * c + q][n]

    lane = lax.broadcasted_iota(jnp.int32, shape, 1)
    level = lax.broadcasted_iota(jnp.int32, shape, 0)
    z_first, z_last = lane == 0, lane == LANES - 1
    y_first, y_last = level == 0, level == 7
    drift = 0.5 * ADVECTION
    half_next, half_prev = (jnp.where(wall, 0.0, 0.5 * CROSS_RATE) for wall in (y_last, y_first))
    inner_next, inner_prev = (jnp.where(wall, 0.0, drift) for wall in (y_last, y_first))

    half = 0.5 * CROSS_RATE

    def source_z(p):
        zero = jnp.zeros(shape, jnp.float32)

        def around(values):
            ahead = [pltpu.roll(x, LANES - 1, 1) for x in values] + [zero]
            behind = [zero] + [pltpu.roll(x, 1, 1) for x in values]
            z_next = [jnp.where(z_last, ahead[c + 1], ahead[c]) for c in range(chunks)]
            z_prev = [jnp.where(z_first, behind[c], behind[c + 1]) for c in range(chunks)]
            return z_next, z_prev

        visc = [half * fv[4, c, p] for c in range(chunks)]
        v_next, v_prev = around(visc)
        face_next = [visc[c] + v_next[c] for c in range(chunks)]
        face_prev = [visc[c] + v_prev[c] for c in range(chunks)]
        speed = [drift * fv[2, c, p] for c in range(chunks)]
        for q in range(2):
            ratio = (1.0, THERMAL_RATIO)[q]
            ahead, behind, centre = [], [], []
            for c in range(chunks):
                faces = [face_next[c], face_prev[c]] if q == 0 else [ratio * face_next[c], ratio * face_prev[c]]
                ahead.append(faces[0] - speed[c])
                behind.append(faces[1] + speed[c])
                centre.append(1.0 - (faces[0] + faces[1]))
            for a in ((0, 1, 2), (3,))[q]:
                own = [fv[a, c, p] for c in range(chunks)]
                z_next, z_prev = around(own)
                for c in range(chunks):
                    src[a, c, p - 1] = centre[c] * own[c] + (ahead[c] * z_next[c] + behind[c] * z_prev[c])

    def source_xy(p, some):
        for c in some:

            def level_pair(a):
                at = ((a * chunks + c) * (rows + 2) + p) * 8
                return flat[pl.ds(at + 1, 8), :], flat[pl.ds(at - 1, 8), :]

            v = fv[4, c, p]
            y_next, y_prev = level_pair(4)
            face_next = half_next * (v + y_next)
            face_prev = half_prev * (v + y_prev)
            own = [fv[a, c, p] for a in range(4)]
            speed_x = drift * own[0]
            speed_next, speed_prev = inner_next * own[1], inner_prev * own[1]
            for q in range(2):
                if q == 1:
                    face_next, face_prev = THERMAL_RATIO * face_next, THERMAL_RATIO * face_prev
                ahead, behind, both = face_next - speed_next, face_prev + speed_prev, face_next + face_prev
                for a in ((0, 1, 2), (3,))[q]:
                    y_next, y_prev = level_pair(a)
                    total = (ahead * y_next + behind * y_prev) - both * own[a]
                    total -= speed_x * (fv[a, c, p + 1] - fv[a, c, p - 1])
                    if a == 2:
                        total += BUOYANCY * own[3]
                    src[a, c, p - 1] += total

    def source_step(i, nothing):
        for n in range(TRIP):
            source_z(2 + TRIP * i + n)
        for n in range(TRIP):
            source_xy(2 + TRIP * i + n, range(chunks))
        return nothing

    trips = (rows - 2) // TRIP
    assert trips * TRIP == rows - 2

    lax.fori_loop(0, EARLY, source_step, 0)
    pl.when(lowest)(lambda: start_when_in(1))
    pl.when(even & jnp.logical_not(lowest))(lambda: start_when_in(0))

    visc_copy.wait_recv()
    inside_left = jnp.where(me == 0, 0.0, 1.0)
    inside_right = jnp.where(me == lines - 1, 0.0, 1.0)
    for c in range(chunks):
        total = fv[4, c, 1] + inside_left * x_left[4, :, pl.ds(c * LANES, LANES)]
        wall = (1.0 - inside_right) * fv[4, c, rows]
        for q in range(2):
            h, e, mass_right = (mass[q, c, n] for n in range(3))
            m, w = matrix_row(c, q, 0, rates(q) * total, h, e)
            mat_out[c, q, 0] = m * e
            mat_out[c, q, 1] = m * h
            mat_out[c, q, 2] = 1.0 + mass_right + w * h + rates(q) * wall

    pl.semaphore_wait(plane_sem, len(column_peers))

    def mat_copy(c, a):
        return pltpu.make_async_remote_copy(
            mat_out.at[c, a // 3], mat_in.at[me], mat_send.at[4 * c + a], mat_recv.at[me],
            device_id={"line": owner_of(c, a)}, device_id_type=MESH)

    slots = [(c, a) for c in range(chunks) for a in range(4)]
    for c, a in slots:

        @pl.when(me != owner_of(c, a))
        def _(c=c, a=a):
            mat_copy(c, a).start()

    mat_in[me] = mat_out[my_chunk, my_field // 3]

    lax.fori_loop(EARLY, trips, source_step, 0)
    source_z(1)
    source_z(rows)

    edge = jnp.where(y_first | y_last, 0.5 * CROSS_RATE, 0.0)
    sign = jnp.where(y_last, -drift, jnp.where(y_first, drift, 0.0))

    def rhs_copy(c, a):
        return pltpu.make_async_remote_copy(
            rhs_out.at[4 * c + a], rhs_in.at[me], rhs_send.at[4 * c + a], rhs_recv.at[me],
            device_id={"line": owner_of(c, a)}, device_id_type=MESH)

    for c in range(chunks):
        for copy in y_copies[c]:
            copy.wait_recv()

        def finished(k):
            def beyond(a):
                low = jnp.broadcast_to(halo_in[0, c, a, pl.ds(k, 1), :], shape)
                high = jnp.broadcast_to(halo_in[1, c, a, pl.ds(k, 1), :], shape)
                return jnp.where(y_last, high, low)

            face = edge * (fv[4, c, k + 1] + beyond(4))
            speed = sign * fv[1, c, k + 1]
            faces = (face, THERMAL_RATIO * face)
            weights = (faces[0] + speed, faces[1] + speed)
            out = []
            for a in range(4):
                q = a // 3
                out.append(src[a, c, k] + (weights[q] * beyond(a) - faces[q] * fv[a, c, k + 1]))
            return out

        def rhs_row(k, carry):
            given = finished(k)
            new = []
            for a in range(4):
                q = a // 3
                passed, gathered = carry[a]
                d = given[a] + passed
                y_ref[c][a, k] = rec[q, c, k] * d
                new.append((m_ref[c][q, k] * d, gathered + w_ref[c][q, k] * d))
            return tuple(new)

        zero = jnp.zeros(shape, jnp.float32)
        ends = ((zero, zero),) * 4
        for k in range(last - 1, 0, -1):
            ends = rhs_row(k, ends)

        for copy in x_copies[c]:
            copy.wait_recv()
        lanes = pl.ds(c * LANES, LANES)
        for a in range(4):
            fv[a, c, 0] = inside_left * x_left[a, :, lanes]
            fv[a, c, rows + 1] = inside_right * x_right[a, :, lanes]
        source_xy(1, (c,))
        source_xy(rows, (c,))
        ends = rhs_row(0, ends)
        at_last = finished(last)
        for a in range(4):
            rhs_out[4 * c + a, 0] = ends[a][0]
            rhs_out[4 * c + a, 1] = ends[a][1] + at_last[a]

        for a in range(4):

            @pl.when(me != owner_of(c, a))
            def _(c=c, a=a):
                rhs_copy(c, a).start()

    rhs_in[me] = rhs_out[my_slot]

    def arrival(source, target, recv, j):
        return pltpu.make_async_remote_copy(
            source, target.at[j], rhs_send.at[0], recv.at[j], device_id={"line": left}, device_id_type=MESH)

    def mat_wait(d, nothing):
        arrival(mat_out.at[0, 0], mat_in, mat_recv, lax.rem(me + d, lines)).wait_recv()
        return nothing

    lax.fori_loop(1, lines, mat_wait, 0)

    def pivot_step(j, before):
        e = mat_in[j, 0]
        r = 1.0 / (e + before)
        m = e * r
        pivots[j, 0] = r
        pivots[j, 1] = m
        ahead = jnp.minimum(j + 1, lines - 1)
        own_mass = mat_in[j, 2] + jnp.where(j + 1 < lines, 1.0, 0.0) * mat_in[ahead, 1]
        return own_mass + m * before

    first = mat_in[0, 0] + (mat_in[0, 2] + mat_in[1, 1])
    final = lax.fori_loop(1, lines, pivot_step, first)
    final = 1.0 / final

    def rhs_wait(d, nothing):
        arrival(rhs_out.at[0], rhs_in, rhs_recv, lax.rem(me + d, lines)).wait_recv()
        return nothing

    lax.fori_loop(1, lines, rhs_wait, 0)
    given = [rhs_in[j, 1] + rhs_in[j + 1, 0] if j + 1 < lines else rhs_in[j, 1] for j in range(lines)]
    for j in range(1, lines):
        given[j] = given[j] + pivots[j, 1] * given[j - 1]
    value = final * given[lines - 1]
    sep[0] = jnp.zeros(shape, jnp.float32)
    sep[lines] = value
    for j in range(lines - 1, 0, -1):
        value = pivots[j, 0] * given[j - 1] + pivots[j, 1] * value
        sep[j] = value

    def sep_copy(j):
        return pltpu.make_async_remote_copy(
            sep.at[pl.ds(j, 2)], bounds.at[my_slot], sep_send.at[j], sep_recv.at[my_slot],
            device_id={"line": j}, device_id_type=MESH)

    for j in range(lines):

        @pl.when(me != j)
        def _(j=j):
            sep_copy(j).start()

    bounds[my_slot] = sep[pl.ds(me, 2)]

    visc_copy.wait_send()
    for group in x_copies + y_copies:
        for copy in group:
            copy.wait_send()
    for c, a in slots:

        @pl.when(me != owner_of(c, a))
        def _(c=c, a=a):
            mat_copy(c, a).wait_send()
            rhs_copy(c, a).wait_send()

    for c in range(chunks):
        for a in range(4):

            @pl.when(me != owner_of(c, a))
            def _(c=c, a=a):
                arrival(sep.at[pl.ds(0, 2)], bounds, sep_recv, 4 * c + a).wait_recv()

        if c < chunks - 1:
            substitute(
                last, y_ref[c], m_ref[c], w_ref[c],
                [(bounds[4 * c + a, 0], bounds[4 * c + a, 1]) for a in range(4)], u_out.at[c])
        else:
            for a in range(4):
                b_out[a] = bounds[4 * c + a]

    for j in range(lines):

        @pl.when(me != j)
        def _(j=j):
            sep_copy(j).wait_send()


def substitute(last, y, m, w, ends, out):
    def row(k, before):
        new = []
        for a in range(4):
            q = a // 3
            u = (y[a, k] + w[q, k] * ends[a][1]) + m[q, k] * before[a]
            out[a, k] = u
            new.append(u)
        return tuple(new)

    def step(i, before):
        for n in range(STEP):
            before = row(1 + STEP * i + n, before)
        return before

    assert (last - 1) % STEP == 0
    first = row(0, tuple(end[0] for end in ends))
    lax.fori_loop(0, (last - 1) // STEP, step, first)
    for a in range(4):
        out[a, last] = ends[a][1]


def back_kernel(rows, chunks, u, y, m, w, b, out, buf, sem):
    copies = []

    def write(c, source):
        copy = pltpu.make_async_copy(source, out.at[:, :, :, pl.ds(c * LANES, LANES)], sem.at[c])
        copy.start()
        copies.append(copy)

    for c in range(chunks - 1):
        write(c, u.at[c])
    substitute(rows - 1, y, m, w, [(b[a, 0], b[a, 1]) for a in range(4)], buf)
    write(chunks - 1, buf)
    for copy in copies:
        copy.wait()


def in_place(array):
    return pltpu.with_memory_space_constraint(array, pltpu.HBM)


def solution(mesh):
    lines, cols = mesh.shape["line"], mesh.shape["col"]

    def local(fields, viscosity):
        _, rows, deep, wide = fields.shape
        chunks = wide // LANES
        assert deep == 8 and 4 * chunks == lines
        f32 = jnp.float32
        tile = (8, LANES)
        vmem = pl.BlockSpec(memory_space=pltpu.VMEM)
        anywhere = pl.BlockSpec(memory_space=pl.ANY)
        dma = pltpu.SemaphoreType.DMA
        parts = pl.pallas_call(
            functools.partial(main_kernel, lines, cols, rows, chunks),
            out_shape=(
                jax.ShapeDtypeStruct((chunks - 1, 4, rows) + tile, f32),
                jax.ShapeDtypeStruct((4, rows) + tile, f32),
                jax.ShapeDtypeStruct((2, rows) + tile, f32),
                jax.ShapeDtypeStruct((2, rows) + tile, f32),
                jax.ShapeDtypeStruct((4, 2) + tile, f32),
            ),
            in_specs=[anywhere, anywhere],
            out_specs=(vmem,) * 5,
            scratch_shapes=[
                pltpu.VMEM((5, chunks, rows + 2) + tile, f32),
                pltpu.VMEM((4, chunks, rows) + tile, f32),
                pltpu.VMEM((chunks - 1, 4, rows) + tile, f32),
                pltpu.VMEM((chunks - 1, 2, rows) + tile, f32),
                pltpu.VMEM((chunks - 1, 2, rows) + tile, f32),
                pltpu.VMEM((2, chunks, rows) + tile, f32),
                pltpu.VMEM((2, chunks, 3) + tile, f32),
                pltpu.VMEM((5, deep, wide), f32),
                pltpu.VMEM((4, deep, wide), f32),
                pltpu.VMEM((2, chunks, 5, rows, LANES), f32),
                pltpu.VMEM((2, chunks, 5, rows, LANES), f32),
                pltpu.VMEM((chunks, 2, 3) + tile, f32),
                pltpu.VMEM((lines, 3) + tile, f32),
                pltpu.VMEM((lines, 2) + tile, f32),
                pltpu.VMEM((lines, 2) + tile, f32),
                pltpu.VMEM((lines + 1,) + tile, f32),
                pltpu.VMEM((lines, 2) + tile, f32),
                pltpu.VMEM((lines, 2) + tile, f32),
                dma((chunks, 2)),
                dma((1 + 2 * chunks,)), dma((1 + 2 * chunks,)), dma((2, chunks)), dma((2, chunks)),
                dma((lines,)), dma((lines,)), dma((lines,)), dma((lines,)), dma((lines,)), dma((lines,)),
                pltpu.SemaphoreType.REGULAR, pltpu.SemaphoreType.REGULAR((2,)),
            ],
            compiler_params=pltpu.CompilerParams(
                collective_id=0, has_side_effects=True, vmem_limit_bytes=40 << 20
            ),
            name="eliminate",
        )(in_place(fields), in_place(viscosity))
        return pl.pallas_call(
            functools.partial(back_kernel, rows, chunks),
            out_shape=jax.ShapeDtypeStruct((4, rows, 8, wide), f32),
            in_specs=[vmem] * 5,
            out_specs=anywhere,
            scratch_shapes=[pltpu.VMEM((4, rows) + tile, f32), dma((chunks,))],
            compiler_params=pltpu.CompilerParams(vmem_limit_bytes=24 << 20),
            name="substitute",
        )(*parts)

    return jax.shard_map(
        local,
        mesh=mesh,
        in_specs=(P(None, "line", "col", None), P("line", "col", None)),
        out_specs=P(None, "line", "col", None),
        check_vma=False,
    )
```

```python
import functools

import jax
import jax.numpy as jnp
from jax import lax
from jax.experimental import pallas as pl
from jax.experimental.pallas import tpu as pltpu
from jax.sharding import PartitionSpec as P

STIFF = 3072.0
THERMAL_RATIO = 0.8
CROSS_RATE = 0.2
ADVECTION = 0.25
BUOYANCY = 2.0
MESH = pl.DeviceIdType.MESH
LANES = 128
STEP = 15
TRIP = 5
EARLY = 2
SWAP = {2: 15, 15: 2}
SIDE = 4


def rates(q):
    return 0.5 * STIFF * (1.0 if q == 0 else THERMAL_RATIO)


def owner_of(c, a):
    near_x, near_y, high_x, high_y = c % 2, c // 2, a % 2, a // 2
    x = (2 + near_x) if high_x else (1 - near_x)
    y = (2 + near_y) if high_y else (1 - near_y)
    return SWAP.get(y * SIDE + x, y * SIDE + x)


def slot_of(me):
    for one, other in SWAP.items():
        if one < other:
            me = jnp.where(me == one, other, jnp.where(me == other, one, me))
    x, y = lax.rem(me, SIDE), me // SIDE
    high_x, high_y = x // 2, y // 2
    near_x = jnp.where(high_x == 1, x - 2, 1 - x)
    near_y = jnp.where(high_y == 1, y - 2, 1 - y)
    return near_x + 2 * near_y, high_x + 2 * high_y


def main_kernel(
    lines, cols, rows, chunks,
    f_hbm, v_hbm,
    u_out, y_end, m_end, w_end, b_out,
    fv, src, y_all, m_all, w_all, rec, mass, x_left, x_right, halo_out, halo_in,
    mat_out, mat_in, rhs_out, rhs_in, sep, bounds, pivots,
    load_sem, x_send, x_recv, y_send, y_recv,
    mat_send, mat_recv, rhs_send, rhs_recv, sep_send, sep_recv, plane_sem, ready_sem,
):
    me = lax.axis_index("line")
    col = lax.axis_index("col")
    right, left = lax.rem(me + 1, lines), lax.rem(me + lines - 1, lines)
    above, below = lax.rem(col + 1, cols), lax.rem(col + cols - 1, cols)
    row_of, place = me // SIDE, lax.rem(me, SIDE)
    my_chunk, my_field = slot_of(me)
    my_slot = 4 * my_chunk + my_field
    last = rows - 1
    shape = (8, LANES)
    y_ref = [y_all.at[c] for c in range(chunks - 1)] + [y_end]
    m_ref = [m_all.at[c] for c in range(chunks - 1)] + [m_end]
    w_ref = [w_all.at[c] for c in range(chunks - 1)] + [w_end]

    barrier = pltpu.get_barrier_semaphore()
    row_peers = [row_of * SIDE + lax.rem(place + d, SIDE) for d in range(1, SIDE)]
    column_peers = [lax.rem(row_of + d, lines // SIDE) * SIDE + place for d in range(1, lines // SIDE)]
    greeted = [{"line": p} for p in [right, left] + row_peers + column_peers]
    for peer in greeted:
        pl.semaphore_signal(barrier, inc=1, device_id=peer, device_id_type=MESH)
    odd = lax.rem(col, 2) == 1

    @pl.when(jnp.logical_not(odd))
    def _():
        for peer in (above, below):
            pl.semaphore_signal(barrier, inc=1, device_id={"col": peer}, device_id_type=MESH)

    loads = []
    own = pl.ds(1, rows)
    for c in range(chunks):
        lanes = pl.ds(c * LANES, LANES)
        loads.append(pltpu.make_async_copy(v_hbm.at[:, :, lanes], fv.at[4, c, own], load_sem.at[c, 0]))
    for c in range(chunks):
        lanes = pl.ds(c * LANES, LANES)
        loads.append(pltpu.make_async_copy(f_hbm.at[:, :, :, lanes], fv.at[pl.ds(0, 4), c, own], load_sem.at[c, 1]))
    for c in range(chunks):
        loads[c].start(priority=1 if c == 0 else 0)
        loads[chunks + c].start(priority=1 if c == 0 else 0)

    @pl.when(odd)
    def _():
        pl.semaphore_wait(barrier, len(greeted) + 2)
        for side, peer in ((1, above), (0, below)):
            pl.semaphore_signal(ready_sem.at[side], inc=1, device_id={"col": peer}, device_id_type=MESH)

    @pl.when(jnp.logical_not(odd))
    def _():
        pl.semaphore_wait(barrier, len(greeted))

    def x_copy(n, source, target, peer):
        return pltpu.make_async_remote_copy(
            source, target, x_send.at[n], x_recv.at[n], device_id={"line": peer}, device_id_type=MESH)

    visc_copy = x_copy(0, v_hbm.at[last], x_left.at[4], right)
    visc_copy.start()
    x_copies = []
    for c in range(chunks):
        lanes = pl.ds(c * LANES, LANES)
        x_copies.append((
            x_copy(1 + c, f_hbm.at[:, last, :, lanes], x_left.at[pl.ds(0, 4), :, lanes], right),
            x_copy(1 + chunks + c, f_hbm.at[:, 0, :, lanes], x_right.at[:, :, lanes], left),
        ))
        for copy in x_copies[c]:
            copy.start()
    y_copies = []
    for c in range(chunks):
        y_copies.append([
            pltpu.make_async_remote_copy(
                halo_out.at[side, c], halo_in.at[side, c], y_send.at[side, c], y_recv.at[side, c],
                device_id={"col": peer}, device_id_type=MESH)
            for side, peer in ((0, above), (1, below))
        ])

    def start_when_in(side):
        pl.semaphore_wait(ready_sem.at[side], 1)
        for group in y_copies:
            group[side].start()

    even, lowest = jnp.logical_not(odd), col == 0

    for peer in column_peers:
        pl.semaphore_signal(plane_sem, inc=1, device_id={"line": peer}, device_id_type=MESH)

    for c in range(chunks):
        fv[4, c, 0] = jnp.zeros(shape, jnp.float32)
        fv[4, c, rows + 1] = jnp.zeros(shape, jnp.float32)

    flat = fv.reshape(5 * chunks * (rows + 2) * 8, LANES)
    for c in range(chunks):
        loads[c].wait()
        loads[chunks + c].wait()
        for a in range(5):
            for side, y in ((0, 7), (1, 0)):
                for g in range(0, rows, 8):
                    at = ((a * chunks + c) * (rows + 2) + 1 + g) * 8 + y
                    halo_out[side, c, a, g : g + 8, :] = flat[pl.ds(at, 8, stride=8), :]

        @pl.when(odd)
        def _(c=c):
            for copy in y_copies[c]:
                copy.start()
    pl.when(lowest)(lambda: start_when_in(0))
    pl.when(even & jnp.logical_not(lowest))(lambda: start_when_in(1))


    def matrix_row(c, q, k, a, h, e):
        r = 1.0 / (a + (h + e))
        m = a * r
        w = e * r
        rec[q, c, k] = r
        m_ref[c][q, k] = m
        w_ref[c][q, k] = w
        return m, w

    def matrix_step(i, carry):
        k = last - 1 - i
        new = []
        for c in range(chunks):
            total = fv[4, c, k + 1] + fv[4, c, k]
            for q in range(2):
                h, e, mass_right = carry[2 * c + q]
                m, w = matrix_row(c, q, k, rates(q) * total, h, e)
                new.append((1.0 + m * h, m * e, mass_right + w * h))
        return tuple(new)

    start = []
    for c in range(chunks):
        total = fv[4, c, rows] + fv[4, c, rows - 1]
        for q in range(2):
            a = rates(q) * total
            start.append((jnp.ones_like(a), a, jnp.zeros_like(a)))
    state = lax.fori_loop(0, last - 1, matrix_step, tuple(start))
    for c in range(chunks):
        for q in range(2):
            for n in range(3):
                mass[q, c, n] = state[2 * c + q][n]

    lane = lax.broadcasted_iota(jnp.int32, shape, 1)
    level = lax.broadcasted_iota(jnp.int32, shape, 0)
    z_first, z_last = lane == 0, lane == LANES - 1
    y_first, y_last = level == 0, level == 7
    drift = 0.5 * ADVECTION
    half_next, half_prev = (jnp.where(wall, 0.0, 0.5 * CROSS_RATE) for wall in (y_last, y_first))
    inner_next, inner_prev = (jnp.where(wall, 0.0, drift) for wall in (y_last, y_first))

    half = 0.5 * CROSS_RATE

    def source_z(p):
        zero = jnp.zeros(shape, jnp.float32)

        def around(values):
            ahead = [pltpu.roll(x, LANES - 1, 1) for x in values] + [zero]
            behind = [zero] + [pltpu.roll(x, 1, 1) for x in values]
            z_next = [jnp.where(z_last, ahead[c + 1], ahead[c]) for c in range(chunks)]
            z_prev = [jnp.where(z_first, behind[c], behind[c + 1]) for c in range(chunks)]
            return z_next, z_prev

        visc = [half * fv[4, c, p] for c in range(chunks)]
        v_next, v_prev = around(visc)
        face_next = [visc[c] + v_next[c] for c in range(chunks)]
        face_prev = [visc[c] + v_prev[c] for c in range(chunks)]
        speed = [drift * fv[2, c, p] for c in range(chunks)]
        for q in range(2):
            ratio = (1.0, THERMAL_RATIO)[q]
            ahead, behind, centre = [], [], []
            for c in range(chunks):
                faces = [face_next[c], face_prev[c]] if q == 0 else [ratio * face_next[c], ratio * face_prev[c]]
                ahead.append(faces[0] - speed[c])
                behind.append(faces[1] + speed[c])
                centre.append(1.0 - (faces[0] + faces[1]))
            for a in ((0, 1, 2), (3,))[q]:
                own = [fv[a, c, p] for c in range(chunks)]
                z_next, z_prev = around(own)
                for c in range(chunks):
                    src[a, c, p - 1] = centre[c] * own[c] + (ahead[c] * z_next[c] + behind[c] * z_prev[c])

    def source_xy(p, some):
        for c in some:

            def level_pair(a):
                at = ((a * chunks + c) * (rows + 2) + p) * 8
                return flat[pl.ds(at + 1, 8), :], flat[pl.ds(at - 1, 8), :]

            v = fv[4, c, p]
            y_next, y_prev = level_pair(4)
            face_next = half_next * (v + y_next)
            face_prev = half_prev * (v + y_prev)
            own = [fv[a, c, p] for a in range(4)]
            speed_x = drift * own[0]
            speed_next, speed_prev = inner_next * own[1], inner_prev * own[1]
            for q in range(2):
                if q == 1:
                    face_next, face_prev = THERMAL_RATIO * face_next, THERMAL_RATIO * face_prev
                ahead, behind, both = face_next - speed_next, face_prev + speed_prev, face_next + face_prev
                for a in ((0, 1, 2), (3,))[q]:
                    y_next, y_prev = level_pair(a)
                    total = (ahead * y_next + behind * y_prev) - both * own[a]
                    total -= speed_x * (fv[a, c, p + 1] - fv[a, c, p - 1])
                    if a == 2:
                        total += BUOYANCY * own[3]
                    src[a, c, p - 1] += total

    def source_step(i, nothing):
        for n in range(TRIP):
            source_z(2 + TRIP * i + n)
        for n in range(TRIP):
            source_xy(2 + TRIP * i + n, range(chunks))
        return nothing

    trips = (rows - 2) // TRIP
    assert trips * TRIP == rows - 2

    lax.fori_loop(0, EARLY, source_step, 0)
    pl.when(lowest)(lambda: start_when_in(1))
    pl.when(even & jnp.logical_not(lowest))(lambda: start_when_in(0))

    visc_copy.wait_recv()
    inside_left = jnp.where(me == 0, 0.0, 1.0)
    inside_right = jnp.where(me == lines - 1, 0.0, 1.0)
    for c in range(chunks):
        total = fv[4, c, 1] + inside_left * x_left[4, :, pl.ds(c * LANES, LANES)]
        wall = (1.0 - inside_right) * fv[4, c, rows]
        for q in range(2):
            h, e, mass_right = (mass[q, c, n] for n in range(3))
            m, w = matrix_row(c, q, 0, rates(q) * total, h, e)
            mat_out[c, q, 0] = m * e
            mat_out[c, q, 1] = m * h
            mat_out[c, q, 2] = 1.0 + mass_right + w * h + rates(q) * wall

    pl.semaphore_wait(plane_sem, len(column_peers))

    def mat_copy(c, a):
        return pltpu.make_async_remote_copy(
            mat_out.at[c, a // 3], mat_in.at[me], mat_send.at[4 * c + a], mat_recv.at[me],
            device_id={"line": owner_of(c, a)}, device_id_type=MESH)

    slots = [(c, a) for c in range(chunks) for a in range(4)]
    for c, a in slots:

        @pl.when(me != owner_of(c, a))
        def _(c=c, a=a):
            mat_copy(c, a).start()

    mat_in[me] = mat_out[my_chunk, my_field // 3]

    lax.fori_loop(EARLY, trips, source_step, 0)
    source_z(1)
    source_z(rows)

    edge = jnp.where(y_first | y_last, 0.5 * CROSS_RATE, 0.0)
    sign = jnp.where(y_last, -drift, jnp.where(y_first, drift, 0.0))

    def rhs_copy(c, a):
        return pltpu.make_async_remote_copy(
            rhs_out.at[4 * c + a], rhs_in.at[me], rhs_send.at[4 * c + a], rhs_recv.at[me],
            device_id={"line": owner_of(c, a)}, device_id_type=MESH)

    def source_ends(c):
        for copy in x_copies[c]:
            copy.wait_recv()
        lanes = pl.ds(c * LANES, LANES)
        for a in range(4):
            fv[a, c, 0] = inside_left * x_left[a, :, lanes]
            fv[a, c, rows + 1] = inside_right * x_right[a, :, lanes]
        source_xy(1, (c,))
        source_xy(rows, (c,))

    for c in range(chunks):
        if c > 0:
            source_ends(c)
        for copy in y_copies[c]:
            copy.wait_recv()

        def finished(k):
            def beyond(a):
                low = jnp.broadcast_to(halo_in[0, c, a, pl.ds(k, 1), :], shape)
                high = jnp.broadcast_to(halo_in[1, c, a, pl.ds(k, 1), :], shape)
                return jnp.where(y_last, high, low)

            face = edge * (fv[4, c, k + 1] + beyond(4))
            speed = sign * fv[1, c, k + 1]
            faces = (face, THERMAL_RATIO * face)
            weights = (faces[0] + speed, faces[1] + speed)
            out = []
            for a in range(4):
                q = a // 3
                out.append(src[a, c, k] + (weights[q] * beyond(a) - faces[q] * fv[a, c, k + 1]))
            return out

        def rhs_row(k, carry):
            given = finished(k)
            new = []
            for a in range(4):
                q = a // 3
                passed, gathered = carry[a]
                d = given[a] + passed
                y_ref[c][a, k] = rec[q, c, k] * d
                new.append((m_ref[c][q, k] * d, gathered + w_ref[c][q, k] * d))
            return tuple(new)

        zero = jnp.zeros(shape, jnp.float32)
        ends = ((zero, zero),) * 4
        for k in range(last - 1, 0, -1):
            ends = rhs_row(k, ends)

        if c == 0:
            source_ends(c)
        ends = rhs_row(0, ends)
        at_last = finished(last)
        for a in range(4):
            rhs_out[4 * c + a, 0] = ends[a][0]
            rhs_out[4 * c + a, 1] = ends[a][1] + at_last[a]

        for a in range(4):

            @pl.when(me != owner_of(c, a))
            def _(c=c, a=a):
                rhs_copy(c, a).start()

    rhs_in[me] = rhs_out[my_slot]

    def arrival(source, target, recv, j):
        return pltpu.make_async_remote_copy(
            source, target.at[j], rhs_send.at[0], recv.at[j], device_id={"line": left}, device_id_type=MESH)

    def mat_wait(d, nothing):
        arrival(mat_out.at[0, 0], mat_in, mat_recv, lax.rem(me + d, lines)).wait_recv()
        return nothing

    lax.fori_loop(1, lines, mat_wait, 0)

    def pivot_step(j, before):
        e = mat_in[j, 0]
        r = 1.0 / (e + before)
        m = e * r
        pivots[j, 0] = r
        pivots[j, 1] = m
        ahead = jnp.minimum(j + 1, lines - 1)
        own_mass = mat_in[j, 2] + jnp.where(j + 1 < lines, 1.0, 0.0) * mat_in[ahead, 1]
        return own_mass + m * before

    first = mat_in[0, 0] + (mat_in[0, 2] + mat_in[1, 1])
    final = lax.fori_loop(1, lines, pivot_step, first)
    final = 1.0 / final

    for j in range(lines):

        @pl.when(me != j)
        def _(j=j):
            arrival(rhs_out.at[0], rhs_in, rhs_recv, j).wait_recv()

    given = [rhs_in[j, 1] + rhs_in[j + 1, 0] if j + 1 < lines else rhs_in[j, 1] for j in range(lines)]
    for j in range(1, lines):
        given[j] = given[j] + pivots[j, 1] * given[j - 1]
    value = final * given[lines - 1]
    sep[0] = jnp.zeros(shape, jnp.float32)
    sep[lines] = value
    for j in range(lines - 1, 0, -1):
        value = pivots[j, 0] * given[j - 1] + pivots[j, 1] * value
        sep[j] = value

    def sep_copy(j):
        return pltpu.make_async_remote_copy(
            sep.at[pl.ds(j, 2)], bounds.at[my_slot], sep_send.at[j], sep_recv.at[my_slot],
            device_id={"line": j}, device_id_type=MESH)

    for j in range(lines):

        @pl.when(me != j)
        def _(j=j):
            sep_copy(j).start()

    bounds[my_slot] = sep[pl.ds(me, 2)]

    visc_copy.wait_send()
    for group in x_copies + y_copies:
        for copy in group:
            copy.wait_send()
    for c, a in slots:

        @pl.when(me != owner_of(c, a))
        def _(c=c, a=a):
            mat_copy(c, a).wait_send()
            rhs_copy(c, a).wait_send()

    for c in range(chunks):
        for a in range(4):

            @pl.when(me != owner_of(c, a))
            def _(c=c, a=a):
                arrival(sep.at[pl.ds(0, 2)], bounds, sep_recv, 4 * c + a).wait_recv()

        if c < chunks - 1:
            substitute(
                last, y_ref[c], m_ref[c], w_ref[c],
                [(bounds[4 * c + a, 0], bounds[4 * c + a, 1]) for a in range(4)], u_out.at[c])
        else:
            for a in range(4):
                b_out[a] = bounds[4 * c + a]

    for j in range(lines):

        @pl.when(me != j)
        def _(j=j):
            sep_copy(j).wait_send()


def substitute(last, y, m, w, ends, out):
    def row(k, before):
        new = []
        for a in range(4):
            q = a // 3
            u = (y[a, k] + w[q, k] * ends[a][1]) + m[q, k] * before[a]
            out[a, k] = u
            new.append(u)
        return tuple(new)

    def step(i, before):
        for n in range(STEP):
            before = row(1 + STEP * i + n, before)
        return before

    assert (last - 1) % STEP == 0
    first = row(0, tuple(end[0] for end in ends))
    lax.fori_loop(0, (last - 1) // STEP, step, first)
    for a in range(4):
        out[a, last] = ends[a][1]


def back_kernel(rows, chunks, u, y, m, w, b, out, buf, sem):
    copies = []

    def write(c, source):
        copy = pltpu.make_async_copy(source, out.at[:, :, :, pl.ds(c * LANES, LANES)], sem.at[c])
        copy.start()
        copies.append(copy)

    for c in range(chunks - 1):
        write(c, u.at[c])
    substitute(rows - 1, y, m, w, [(b[a, 0], b[a, 1]) for a in range(4)], buf)
    write(chunks - 1, buf)
    for copy in copies:
        copy.wait()


def in_place(array):
    return pltpu.with_memory_space_constraint(array, pltpu.HBM)


def solution(mesh):
    lines, cols = mesh.shape["line"], mesh.shape["col"]

    def local(fields, viscosity):
        _, rows, deep, wide = fields.shape
        chunks = wide // LANES
        assert deep == 8 and 4 * chunks == lines
        f32 = jnp.float32
        tile = (8, LANES)
        vmem = pl.BlockSpec(memory_space=pltpu.VMEM)
        anywhere = pl.BlockSpec(memory_space=pl.ANY)
        dma = pltpu.SemaphoreType.DMA
        parts = pl.pallas_call(
            functools.partial(main_kernel, lines, cols, rows, chunks),
            out_shape=(
                jax.ShapeDtypeStruct((chunks - 1, 4, rows) + tile, f32),
                jax.ShapeDtypeStruct((4, rows) + tile, f32),
                jax.ShapeDtypeStruct((2, rows) + tile, f32),
                jax.ShapeDtypeStruct((2, rows) + tile, f32),
                jax.ShapeDtypeStruct((4, 2) + tile, f32),
            ),
            in_specs=[anywhere, anywhere],
            out_specs=(vmem,) * 5,
            scratch_shapes=[
                pltpu.VMEM((5, chunks, rows + 2) + tile, f32),
                pltpu.VMEM((4, chunks, rows) + tile, f32),
                pltpu.VMEM((chunks - 1, 4, rows) + tile, f32),
                pltpu.VMEM((chunks - 1, 2, rows) + tile, f32),
                pltpu.VMEM((chunks - 1, 2, rows) + tile, f32),
                pltpu.VMEM((2, chunks, rows) + tile, f32),
                pltpu.VMEM((2, chunks, 3) + tile, f32),
                pltpu.VMEM((5, deep, wide), f32),
                pltpu.VMEM((4, deep, wide), f32),
                pltpu.VMEM((2, chunks, 5, rows, LANES), f32),
                pltpu.VMEM((2, chunks, 5, rows, LANES), f32),
                pltpu.VMEM((chunks, 2, 3) + tile, f32),
                pltpu.VMEM((lines, 3) + tile, f32),
                pltpu.VMEM((lines, 2) + tile, f32),
                pltpu.VMEM((lines, 2) + tile, f32),
                pltpu.VMEM((lines + 1,) + tile, f32),
                pltpu.VMEM((lines, 2) + tile, f32),
                pltpu.VMEM((lines, 2) + tile, f32),
                dma((chunks, 2)),
                dma((1 + 2 * chunks,)), dma((1 + 2 * chunks,)), dma((2, chunks)), dma((2, chunks)),
                dma((lines,)), dma((lines,)), dma((lines,)), dma((lines,)), dma((lines,)), dma((lines,)),
                pltpu.SemaphoreType.REGULAR, pltpu.SemaphoreType.REGULAR((2,)),
            ],
            compiler_params=pltpu.CompilerParams(
                collective_id=0, has_side_effects=True, vmem_limit_bytes=40 << 20
            ),
            name="eliminate",
        )(in_place(fields), in_place(viscosity))
        return pl.pallas_call(
            functools.partial(back_kernel, rows, chunks),
            out_shape=jax.ShapeDtypeStruct((4, rows, 8, wide), f32),
            in_specs=[vmem] * 5,
            out_specs=anywhere,
            scratch_shapes=[pltpu.VMEM((4, rows) + tile, f32), dma((chunks,))],
            compiler_params=pltpu.CompilerParams(vmem_limit_bytes=24 << 20),
            name="substitute",
        )(*parts)

    return jax.shard_map(
        local,
        mesh=mesh,
        in_specs=(P(None, "line", "col", None), P("line", "col", None)),
        out_specs=P(None, "line", "col", None),
        check_vma=False,
    )
```
